256 devices in a mesh: row: 16 (over z, core), col: 16 (over x, y).
Axes of the slice: x: 4, y: 4, z: 8, core: 2. Of those that a mesh axis runs over, the one named last changes fastest.
Arguments:
- cost_tiles: float32 [16, 16, 64, 128, 128], P('row', 'col'), may hold values from 0 to 66
- tile_rows: int32 [16, 16, 64], P('row', 'col'), may hold values from 0 to 127, as said below
- tile_cols: int32 [16, 16, 64], P('row', 'col'), may hold values from 0 to 127
- tile_count: int32 [16, 16], P('row', 'col'), may hold values from 16 to 64, as said below
- source_logmass: float32 [262144], P('row'), may hold values from -3 to 0
- target_logmass: float32 [262144], P('col'), may hold values from -103 to -100
- target_init: float32 [262144], P('col'), may hold values from -2 to 14
Outputs:
- source_potential: float32 [262144], P('row')
- target_potential: float32 [262144], P('col')
The draws below stay inside these ranges and needn't reach their ends.
Inputs may be any that keep to these rules, and one draw needn't show every extreme that they name: Among the first tile_count slots of a device all (tile_rows, tile_cols) pairs differ; every source block of a row shard appears in such a slot of some device of that shard, and every target block of a col shard likewise. Slots at tile_count or later hold pairs to be ignored. `tile_count`: some device has all 64 slots in use in every draw.
All inputs are finite; a program needn't handle non-finite values.
Results may differ from the reference program's by a relative error of at most 0.00019.
Values sent between devices are 32-bit elements; how exact they have to be, the bound alone decides.
No kernel may reach another device: no remote copies, remote signals or barrier semaphores. Data moves between devices by JAX's collectives and lax.ppermute only.
A program may use at most 64 MiB of HBM per device.

```python
import jax
import jax.numpy as jnp
from jax import lax

BLOCK = 128
RB = 128
CB = 128
CAP = 64
ITERS = 2
NSRC = 262144
NTGT = 262144
N_ROW = 16
N_COL = 16


def tile_lists(key):
    base = jax.random.fold_in(key, 7)
    ndev = N_ROW * N_COL
    shard_r = jnp.arange(ndev) // N_COL
    shard_c = jnp.arange(ndev) % N_COL
    cover_r = RB // N_COL
    cover_c = CB // N_ROW
    cover = max(cover_r, cover_c)
    keys = jax.random.split(jax.random.fold_in(base, 1), ndev)
    ranks = jax.vmap(lambda single: jax.random.permutation(single, RB * CB))(keys).astype(jnp.int32)
    steps = jnp.arange(cover)
    forced = (shard_c[:, None] * cover_r + steps[None, :] % cover_r) * CB + shard_r[:, None] * cover_c + steps[None, :] % cover_c
    lanes = jnp.arange(ndev)[:, None] + jnp.zeros((1, cover), jnp.int32)
    ranks = ranks.at[lanes, forced].set(steps[None, :] - cover)
    order = jnp.argsort(ranks, axis=1, stable=True)[:, :CAP].astype(jnp.int32)
    rows = (order // CB).reshape(N_ROW, N_COL, CAP)
    cols = (order % CB).reshape(N_ROW, N_COL, CAP)
    lowest = max(cover, CAP // 4)
    span = CAP - lowest
    first = jax.random.randint(jax.random.fold_in(base, 2), (ndev,), 0, span + 1)
    second = jax.random.randint(jax.random.fold_in(base, 3), (ndev,), 0, span + 1)
    counts = lowest + first * second // max(span, 1)
    busiest = jax.random.randint(jax.random.fold_in(base, 4), (), 0, ndev)
    counts = counts.at[busiest].set(CAP).astype(jnp.int32)
    return (rows, cols, counts.reshape(N_ROW, N_COL))


def draw_tile_rows(key, part):
    return tile_lists(key)[0]


def draw_tile_cols(key, part):
    return tile_lists(key)[1]


def draw_tile_count(key, part):
    return tile_lists(key)[2]


def draw_cost_tiles(key, part):
    shape = (N_ROW, N_COL, CAP, BLOCK, BLOCK)
    rows, cols, counts = tile_lists(key)
    first = jax.random.fold_in(key, 11)
    row_lift = jax.random.uniform(jax.random.fold_in(key, 13), (NSRC,), jnp.float32, 0.0, 30.0)
    col_lift = jax.random.uniform(jax.random.fold_in(key, 14), (NTGT,), jnp.float32, 0.0, 30.0)
    shard_r = jnp.arange(N_ROW).reshape(N_ROW, 1, 1, 1)
    shard_c = jnp.arange(N_COL).reshape(1, N_COL, 1, 1)
    lanes = jnp.arange(BLOCK).reshape(1, 1, 1, BLOCK)
    source_index = ((shard_r * RB + rows[..., None]) * BLOCK + lanes).astype(jnp.int32)
    target_index = ((shard_c * CB + cols[..., None]) * BLOCK + lanes).astype(jnp.int32)
    base = jax.random.uniform(first, shape, jnp.float32, 0.0, 6.0)
    return base + row_lift[source_index][..., :, None] + col_lift[target_index][..., None, :]


def draw_target_init(key, part):
    first = jax.random.fold_in(key, 21)
    drawn = jax.random.uniform(first, (NTGT,), jnp.float32, -2.0, 2.0)
    return drawn


def shard_levels(key, shape, shards, smallest, high):
    factor_of, own = 1.0, jax.random.fold_in(key, 6)
    for position, blocks in shards:
        steps = jnp.exp(jax.random.uniform(jax.random.fold_in(own, position), (blocks,), jnp.float32, smallest / len(shards), high / len(shards)))
        factor_of = factor_of * jnp.repeat(steps, shape[position] // blocks).reshape([-1 if axis == position else 1 for axis in range(len(shape))])
    return factor_of


def setup_inputs(seed: int = 0) -> dict:
    seeds = jax.random.split(jax.random.key(seed), 8)
    cost_tiles = draw_cost_tiles(jax.random.fold_in(seeds[7], 71), 0)
    tile_rows = draw_tile_rows(jax.random.fold_in(seeds[7], 71), 0)
    tile_cols = draw_tile_cols(jax.random.fold_in(seeds[7], 71), 0)
    tile_count = draw_tile_count(jax.random.fold_in(seeds[7], 71), 0)
    source_logmass = jnp.clip(-3.0 + 3.0 * jax.random.uniform(seeds[4], (NSRC,), jnp.float32) ** shard_levels(seeds[4], (NSRC,), ((0, 16),), -0.2, 0.2), -3.0, 0.0)
    target_logmass = jnp.clip(-103.0 + 3.0 * jax.random.uniform(seeds[5], (NTGT,), jnp.float32) ** shard_levels(seeds[5], (NTGT,), ((0, 16),), -0.2, 0.2), -103.0, -100.0)
    target_init = draw_target_init(jax.random.fold_in(seeds[7], 71), 0)
    return {"cost_tiles": cost_tiles, "tile_rows": tile_rows, "tile_cols": tile_cols, "tile_count": tile_count, "source_logmass": source_logmass, "target_logmass": target_logmass, "target_init": target_init}


EPS = 0.1


def side_lse(cost, pot, gather_ids, seg_ids, valid, nseg, rows_side):
    blocks = pot.reshape(-1, BLOCK)
    red = 2 if rows_side else 1

    def scores(tiles, gid):
        part = blocks[gid]
        if rows_side:
            return (part[:, None, :] - tiles) / EPS
        return (part[:, :, None] - tiles) / EPS

    def peak(args):
        tiles, gid = args
        return jnp.max(scores(tiles, gid), axis=red)

    tmax = lax.map(peak, (cost, gather_ids))
    tmax = jnp.where(valid[:, :, None], tmax, -jnp.inf)
    ids = jnp.where(valid, seg_ids, 0).reshape(-1).astype(jnp.int32)
    top = jax.ops.segment_max(tmax.reshape(-1, BLOCK), ids, num_segments=nseg)

    def total(args):
        tiles, gid, sid, okay = args
        shift = top[sid]
        shift = jnp.where(okay[:, None], shift, 0.0)
        if rows_side:
            expo = jnp.exp(scores(tiles, gid) - shift[:, :, None])
        else:
            expo = jnp.exp(scores(tiles, gid) - shift[:, None, :])
        return jnp.where(okay[:, None], jnp.sum(expo, axis=red), 0.0)

    sums = lax.map(total, (cost, gather_ids, seg_ids, valid))
    mass = jax.ops.segment_sum(sums.reshape(-1, BLOCK), ids, num_segments=nseg)
    return (top + jnp.log(mass)).reshape(-1)


def reference(cost_tiles, tile_rows, tile_cols, tile_count, source_logmass, target_logmass, target_init):
    ndev = N_ROW * N_COL
    cost = cost_tiles.reshape(ndev, CAP, BLOCK, BLOCK)
    shard_r = (jnp.arange(ndev) // N_COL).astype(jnp.int32)
    shard_c = (jnp.arange(ndev) % N_COL).astype(jnp.int32)
    grow = (tile_rows.reshape(ndev, CAP) + shard_r[:, None] * RB).astype(jnp.int32)
    gcol = (tile_cols.reshape(ndev, CAP) + shard_c[:, None] * CB).astype(jnp.int32)
    valid = jnp.arange(CAP)[None, :] < tile_count.reshape(-1)[:, None]
    target_potential = target_init
    source_potential = source_logmass
    for step in range(ITERS):
        source_potential = EPS * source_logmass - EPS * side_lse(cost, target_potential, gcol, grow, valid, N_ROW * RB, True)
        target_potential = EPS * target_logmass - EPS * side_lse(cost, source_potential, grow, gcol, valid, N_COL * CB, False)
    return source_potential, target_potential
```

```python
import jax
import jax.numpy as jnp
import numpy as np
from jax import lax
from jax.experimental import pallas as pl
from jax.experimental.pallas import tpu as pltpu
from jax.sharding import Mesh
from jax.sharding import PartitionSpec as P

ITERS = 2
EPS = 0.1
LN2 = float(np.log(2.0))
UNIT = 1.0 / (EPS * LN2)
BACK = EPS * LN2
NONE = -1.0e30
LANES = 128
WAYS = 4
CHUNK = 8


def lse2(parts):
    top = jnp.max(parts, axis=0)
    return top + jnp.log2(jnp.sum(jnp.exp2(parts - top[None]), axis=0))


def merge_slots(values, seg_ref, count, peak, mass):
    slots = values.shape[0]
    nseg = peak.shape[1] - 8

    def home(s):
        return jnp.where(s < count, seg_ref[s], nseg)

    peak[...] = jnp.full(peak.shape, NONE, jnp.float32)
    mass[...] = jnp.zeros(mass.shape, jnp.float32)
    for s in range(slots):
        at = (s % WAYS, pl.ds(home(s), 1), slice(None))
        peak[at] = jnp.maximum(peak[at], values[pl.ds(s, 1), :])
    top = peak[0]
    for way in range(1, WAYS):
        top = jnp.maximum(top, peak[way])
    peak[0] = top
    for s in range(slots):
        row = pl.ds(home(s), 1)
        at = (s % WAYS, row, slice(None))
        mass[at] = mass[at] + jnp.exp2(values[pl.ds(s, 1), :] - peak[0, row, :])
    total = mass[0]
    for way in range(1, WAYS):
        total = total + mass[way]
    dense = jnp.maximum(top + jnp.log2(total), NONE)
    return dense[:nseg]


def fetch_all(cost_hbm, cost, sems):
    for k in range(cost.shape[0] // CHUNK):
        at = pl.ds(k * CHUNK, CHUNK)
        pltpu.make_async_copy(cost_hbm.at[at], cost.at[at], sems.at[k]).start()


def fetch_wait(cost_hbm, cost, sems, k):
    at = pl.ds(k * CHUNK, CHUNK)
    pltpu.make_async_copy(cost_hbm.at[at], cost.at[at], sems.at[k]).wait()


def rows_side(rows, cols, count, cost_hbm, cost, sems, pot, values, peak, mass):
    slots = cost.shape[0]
    lane = lax.broadcasted_iota(jnp.int32, (LANES, LANES), 1)

    def one(s, held):
        part = pot[pl.ds(cols[s], 1), :]
        scores = (part - cost[s]) * UNIT
        top = jnp.max(scores, axis=1, keepdims=True)
        total = jnp.sum(jnp.exp2(scores - top), axis=1, keepdims=True)
        return jnp.where(lane == s, top + jnp.log2(total), held)

    def chunk(k, held):
        fetch_wait(cost_hbm, cost, sems, k)
        for i in range(CHUNK):
            held = one(k * CHUNK + i, held)
        return held

    held = lax.fori_loop(0, slots // CHUNK, chunk, jnp.zeros((LANES, LANES), jnp.float32))
    values[...] = held.T[:slots]
    return merge_slots(values, rows, count, peak, mass)


def cols_side(rows, cols, count, cost_hbm, cost, sems, pot, values, peak, mass):
    slots = cost.shape[0]
    eye = lax.broadcasted_iota(jnp.int32, (LANES, LANES), 1) == lax.broadcasted_iota(
        jnp.int32, (LANES, LANES), 0
    )

    def one(s):
        part = pot[pl.ds(rows[s], 1), :]
        upright = jnp.sum(jnp.where(eye, part, 0.0), axis=1, keepdims=True)
        scores = (upright - cost[s]) * UNIT
        top = jnp.max(scores, axis=0, keepdims=True)
        total = jnp.sum(jnp.exp2(scores - top), axis=0, keepdims=True)
        values[pl.ds(s, 1), :] = top + jnp.log2(total)

    def chunk(k, carry):
        fetch_wait(cost_hbm, cost, sems, k)
        for i in range(CHUNK):
            one(k * CHUNK + i)
        return carry

    lax.fori_loop(0, slots // CHUNK, chunk, 0)
    return merge_slots(values, cols, count, peak, mass)


def first_rows_kernel(rows, cols, count, cost_hbm, pot_in, out, cost, sems, values, peak, mass):
    fetch_all(cost_hbm, cost, sems)
    out[...] = rows_side(
        rows, cols, count[0, 0], cost_hbm, cost, sems, pot_in, values, peak, mass
    )


def rows_kernel(
    rows, cols, count, core, cost_hbm, mine, other, logmass, out, cost, sems, values, peak, mass, pot
):
    fetch_all(cost_hbm, cost, sems)
    half = mine.shape[0]
    at = pl.multiple_of(core[0] * half, half)
    away = pl.multiple_of((1 - core[0]) * half, half)
    pot[pl.ds(at, half), :] = EPS * logmass[pl.ds(at, half), :] - BACK * mine[...]
    pot[pl.ds(away, half), :] = EPS * logmass[pl.ds(away, half), :] - BACK * other[...]
    out[...] = rows_side(
        rows, cols, count[0, 0], cost_hbm, cost, sems, pot, values, peak, mass
    )


def cols_kernel(
    rows, cols, count, core, cost_hbm, parts, logmass, pot, keep, send, cost, sems, values, peak, mass, dense
):
    fetch_all(cost_hbm, cost, sems)
    pot[...] = EPS * logmass[...] - BACK * lse2(parts[...])
    dense[...] = cols_side(
        rows, cols, count[0, 0], cost_hbm, cost, sems, pot, values, peak, mass
    )
    half = keep.shape[0]
    keep[...] = dense[pl.ds(pl.multiple_of(core[0] * half, half), half), :]
    send[...] = dense[pl.ds(pl.multiple_of((1 - core[0]) * half, half), half), :]


def call(kernel, name, smem, hbm, vmem, outs, nseg, extra):
    slots = hbm.shape[0]
    smem_spec = pl.BlockSpec(memory_space=pltpu.SMEM)
    vmem_spec = pl.BlockSpec(memory_space=pltpu.VMEM)
    single = len(outs) == 1
    return pl.pallas_call(
        kernel,
        name=name,
        out_shape=outs[0] if single else outs,
        in_specs=[smem_spec] * len(smem) + [pl.BlockSpec(memory_space=pl.ANY)] + [vmem_spec] * len(vmem),
        out_specs=vmem_spec if single else tuple(vmem_spec for _ in outs),
        scratch_shapes=[
            pltpu.VMEM(hbm.shape, jnp.float32),
            pltpu.SemaphoreType.DMA((slots // CHUNK,)),
            pltpu.VMEM((slots, LANES), jnp.float32),
            pltpu.VMEM((WAYS, nseg + 8, LANES), jnp.float32),
            pltpu.VMEM((WAYS, nseg + 8, LANES), jnp.float32),
            *extra,
        ],
        compiler_params=pltpu.CompilerParams(vmem_limit_bytes=24 << 20),
    )(*smem, hbm, *vmem)


def to_all(value, axes, peers):
    copies = jnp.broadcast_to(value[None], (peers, *value.shape))
    return lax.all_to_all(copies, axes, 0, 0, tiled=True)


def local(
    cost_tiles, tile_rows, tile_cols, tile_count, source_logmass, target_logmass, target_init
):
    cost = cost_tiles.reshape(cost_tiles.shape[2:])
    rows = tile_rows.reshape(-1)
    cols = tile_cols.reshape(-1)
    count = tile_count.reshape(1, 1)
    srcmass = source_logmass.reshape(-1, LANES)
    tgtmass = target_logmass.reshape(-1, LANES)
    nsrc, ntgt = srcmass.shape[0], tgtmass.shape[0]
    ncol = lax.axis_size("col")
    nz = lax.axis_size("z")
    core = lax.axis_index("core")
    core1 = core.reshape(1).astype(jnp.int32)
    swap = [(0, 1), (1, 0)]

    def f32(*shape):
        return jax.ShapeDtypeStruct(shape, jnp.float32)

    mine = other = None
    for step in range(ITERS):
        if step == 0:
            dense = call(
                first_rows_kernel, "first_rows", (rows, cols, count), cost,
                (target_init.reshape(-1, LANES),), (f32(nsrc, LANES),), nsrc, (),
            )
        else:
            dense = call(
                rows_kernel, "rows_half", (rows, cols, count, core1), cost,
                (mine, other, tgtmass), (f32(nsrc, LANES),), nsrc,
                (pltpu.VMEM((ntgt, LANES), jnp.float32),),
            )
        parts = to_all(dense, "col", ncol).reshape(ncol, nsrc, LANES)
        source, keep, send = call(
            cols_kernel, "cols_half", (rows, cols, count, core1), cost,
            (parts, srcmass), (f32(nsrc, LANES), f32(ntgt // 2, LANES), f32(ntgt // 2, LANES)),
            ntgt, (pltpu.VMEM((ntgt, LANES), jnp.float32),),
        )
        got = lax.ppermute(send, "core", swap)
        top = jnp.maximum(keep, got)
        chip = top + jnp.log2(1.0 + jnp.exp2(-jnp.abs(keep - got)))
        mine = lse2(to_all(chip, "z", nz).reshape(nz, ntgt // 2, LANES))
        other = lax.ppermute(mine, "core", swap)
    first = jnp.where(core == 0, mine, other)
    second = jnp.where(core == 0, other, mine)
    target = EPS * tgtmass - BACK * jnp.concatenate([first, second], axis=0)
    return (source.reshape(-1), target.reshape(-1))


def solution(mesh):
    nrow, ncol = mesh.devices.shape
    cores = 2
    finer = Mesh(mesh.devices.reshape(nrow // cores, cores, ncol), ("z", "core", "col"))
    row = ("z", "core")
    return jax.shard_map(
        local,
        mesh=finer,
        in_specs=(
            P(row, "col", None, None, None),
            P(row, "col", None),
            P(row, "col", None),
            P(row, "col"),
            P(row),
            P("col"),
            P("col"),
        ),
        out_specs=(P(row), P("col")),
        check_vma=False,
    )
```

```python
import jax
import jax.numpy as jnp
import numpy as np
from jax import lax
from jax.experimental import pallas as pl
from jax.experimental.pallas import tpu as pltpu
from jax.sharding import Mesh
from jax.sharding import PartitionSpec as P

ITERS = 2
EPS = 0.1
LN2 = float(np.log(2.0))
UNIT = 1.0 / (EPS * LN2)
BACK = EPS * LN2
NONE = -1.0e30
LANES = 128
WAYS = 4
CHUNK = 8
LIMIT = 24 << 20


def lse2(parts):
    top = jnp.max(parts, axis=0)
    return top + jnp.log2(jnp.sum(jnp.exp2(parts - top[None]), axis=0))


def merge_slots(values, seg_ref, count, peak, mass):
    slots = values.shape[0]
    nseg = peak.shape[1] - 8

    def home(s):
        return jnp.where(s < count, seg_ref[s], nseg)

    peak[...] = jnp.full(peak.shape, NONE, jnp.float32)
    mass[...] = jnp.zeros(mass.shape, jnp.float32)
    for s in range(slots):
        at = (s % WAYS, pl.ds(home(s), 1), slice(None))
        peak[at] = jnp.maximum(peak[at], values[pl.ds(s, 1), :])
    top = peak[0]
    for way in range(1, WAYS):
        top = jnp.maximum(top, peak[way])
    peak[0] = top
    for s in range(slots):
        row = pl.ds(home(s), 1)
        at = (s % WAYS, row, slice(None))
        mass[at] = mass[at] + jnp.exp2(values[pl.ds(s, 1), :] - peak[0, row, :])
    total = mass[0]
    for way in range(1, WAYS):
        total = total + mass[way]
    dense = jnp.maximum(top + jnp.log2(total), NONE)
    return dense[:nseg]


def one_row_tile(part, tile):
    scores = ((part - tile) * UNIT).T
    top = jnp.max(scores, axis=0, keepdims=True)
    return top + jnp.log2(jnp.sum(jnp.exp2(scores - top), axis=0, keepdims=True))


def one_col_tile(part, tile):
    upright = jnp.broadcast_to(part, tile.shape).T
    scores = (upright - tile) * UNIT
    top = jnp.max(scores, axis=0, keepdims=True)
    return top + jnp.log2(jnp.sum(jnp.exp2(scores - top), axis=0, keepdims=True))


def fetch(cost_in, cost, sems):
    copies = []
    for k in range(cost.shape[0] // CHUNK):
        at = pl.ds(k * CHUNK, CHUNK)
        copies.append(pltpu.make_async_copy(cost_in.at[at], cost.at[at], sems.at[k]))
        copies[-1].start()
    return copies


def tiles(tile_lse, ids, chunks, cost, pot, values):
    for k, chunk in enumerate(chunks):
        chunk.wait()
        for s in range(k * CHUNK, (k + 1) * CHUNK):
            values[pl.ds(s, 1), :] = tile_lse(pot[pl.ds(ids[s], 1), :], cost[s])


def start_all(pairs, sems):
    copies = [pltpu.make_async_copy(src, dst, sems.at[k]) for k, (src, dst) in enumerate(pairs)]
    for copy in copies:
        copy.start()
    return copies


def first_rows_kernel(
    rows_in, cols_in, cost_in, pot_in, count, core, out, cost, rows, cols, pot, sems, cost_sems, values, peak, mass
):
    small = start_all(((cols_in, cols), (pot_in, pot), (rows_in, rows)), sems)
    chunks = fetch(cost_in, cost, cost_sems)
    small[0].wait()
    small[1].wait()
    tiles(one_row_tile, cols, chunks, cost, pot, values)
    small[2].wait()
    out[...] = merge_slots(values, rows, count[0, 0], peak, mass)


def rows_kernel(
    rows_in, cols_in, cost_in, count, core, mine, other, logmass, out, cost, rows, cols, pot, sems, cost_sems, values, peak, mass
):
    small = start_all(((cols_in, cols), (rows_in, rows)), sems)
    chunks = fetch(cost_in, cost, cost_sems)
    half = mine.shape[0]
    at = pl.multiple_of(core[0] * half, half)
    away = pl.multiple_of((1 - core[0]) * half, half)
    pot[pl.ds(at, half), :] = EPS * logmass[pl.ds(at, half), :] - BACK * mine[...]
    pot[pl.ds(away, half), :] = EPS * logmass[pl.ds(away, half), :] - BACK * other[...]
    for copy in small:
        copy.wait()
    tiles(one_row_tile, cols, chunks, cost, pot, values)
    out[...] = merge_slots(values, rows, count[0, 0], peak, mass)


def cols_kernel(
    rows_in, cols_in, cost_in, count, core, parts, logmass, pot, keep, send, cost, rows, cols, dense, sems, cost_sems, values, peak, mass
):
    small = start_all(((rows_in, rows), (cols_in, cols)), sems)
    chunks = fetch(cost_in, cost, cost_sems)
    pot[...] = EPS * logmass[...] - BACK * lse2(parts[...])
    for copy in small:
        copy.wait()
    tiles(one_col_tile, rows, chunks, cost, pot, values)
    dense[...] = merge_slots(values, cols, count[0, 0], peak, mass)
    half = keep.shape[0]
    keep[...] = dense[pl.ds(pl.multiple_of(core[0] * half, half), half), :]
    send[...] = dense[pl.ds(pl.multiple_of((1 - core[0]) * half, half), half), :]


def call(kernel, name, anywhere, smem, vmem, outs, slots, nseg):
    held = pl.BlockSpec(memory_space=pltpu.VMEM)
    specs = [pl.BlockSpec(memory_space=pl.ANY)] * len(anywhere)
    specs += [pl.BlockSpec(memory_space=pltpu.SMEM)] * len(smem) + [held] * len(vmem)
    single = len(outs) == 1
    return pl.pallas_call(
        kernel,
        name=name,
        out_shape=outs[0] if single else outs,
        in_specs=specs,
        out_specs=held if single else tuple(held for _ in outs),
        scratch_shapes=[
            pltpu.VMEM((slots, LANES, LANES), jnp.float32),
            pltpu.SMEM((slots,), jnp.int32),
            pltpu.SMEM((slots,), jnp.int32),
            pltpu.VMEM((nseg, LANES), jnp.float32),
            pltpu.SemaphoreType.DMA((3,)),
            pltpu.SemaphoreType.DMA((slots // CHUNK,)),
            pltpu.VMEM((slots, LANES), jnp.float32),
            pltpu.VMEM((WAYS, nseg + 8, LANES), jnp.float32),
            pltpu.VMEM((WAYS, nseg + 8, LANES), jnp.float32),
        ],
        compiler_params=pltpu.CompilerParams(vmem_limit_bytes=LIMIT),
    )(*[pltpu.with_memory_space_constraint(x, pltpu.HBM) for x in anywhere], *smem, *vmem)


def to_all(value, axes, peers):
    copies = jnp.broadcast_to(value[None], (peers, *value.shape))
    return lax.all_to_all(copies, axes, 0, 0, tiled=True)


def local(
    cost_tiles, tile_rows, tile_cols, tile_count, source_logmass, target_logmass, target_init
):
    cost = cost_tiles.reshape(cost_tiles.shape[2:])
    rows = tile_rows.reshape(-1)
    cols = tile_cols.reshape(-1)
    count = tile_count.reshape(1, 1)
    srcmass = source_logmass.reshape(-1, LANES)
    tgtmass = target_logmass.reshape(-1, LANES)
    nsrc, ntgt = srcmass.shape[0], tgtmass.shape[0]
    ncol = lax.axis_size("col")
    nz = lax.axis_size("z")
    core = lax.axis_index("core")
    core1 = core.reshape(1).astype(jnp.int32)
    swap = [(0, 1), (1, 0)]

    def f32(*shape):
        return jax.ShapeDtypeStruct(shape, jnp.float32)

    mine = other = None
    slots = cost.shape[0]
    tiled = (rows, cols, cost)
    full, half = f32(nsrc, LANES), f32(ntgt // 2, LANES)
    for step in range(ITERS):
        if step == 0:
            dense = call(
                first_rows_kernel, "first_rows", (*tiled, target_init.reshape(-1, LANES)), (count, core1), (),
                (pltpu.VMEM((nsrc, LANES), jnp.float32),), slots, nsrc,
            )
        else:
            dense = call(
                rows_kernel, "rows_half", tiled, (count, core1), (mine, other, tgtmass), (full,), slots, nsrc
            )
        parts = to_all(dense, "col", ncol).reshape(ncol, nsrc, LANES)
        source, keep, send = call(
            cols_kernel, "cols_half", tiled, (count, core1), (parts, srcmass), (full, half, half), slots, ntgt
        )
        got = lax.ppermute(send, "core", swap)
        top = jnp.maximum(keep, got)
        chip = top + jnp.log2(1.0 + jnp.exp2(-jnp.abs(keep - got)))
        mine = lse2(to_all(chip, "z", nz).reshape(nz, ntgt // 2, LANES))
        other = lax.ppermute(mine, "core", swap)
    first = jnp.where(core == 0, mine, other)
    second = jnp.where(core == 0, other, mine)
    target = EPS * tgtmass - BACK * jnp.concatenate([first, second], axis=0)
    return (source.reshape(-1), target.reshape(-1))


def solution(mesh):
    nrow, ncol = mesh.devices.shape
    cores = 2
    finer = Mesh(mesh.devices.reshape(nrow // cores, cores, ncol), ("z", "core", "col"))
    row = ("z", "core")
    return jax.shard_map(
        local,
        mesh=finer,
        in_specs=(
            P(row, "col", None, None, None),
            P(row, "col", None),
            P(row, "col", None),
            P(row, "col"),
            P(row),
            P("col"),
            P("col"),
        ),
        out_specs=(P(row), P("col")),
        check_vma=False,
    )
```

```python
import jax
import jax.numpy as jnp
import numpy as np
from jax import lax
from jax.experimental import pallas as pl
from jax.experimental.pallas import tpu as pltpu
from jax.sharding import Mesh
from jax.sharding import PartitionSpec as P

ITERS = 2
EPS = 0.1
LN2 = float(np.log(2.0))
UNIT = 1.0 / (EPS * LN2)
BACK = EPS * LN2
NONE = -1.0e30
LANES = 128
CHUNK = 8
LIMIT = 24 << 20


def pieces(x):
    high = x.astype(jnp.bfloat16)
    rest = x - high.astype(jnp.float32)
    middle = rest.astype(jnp.bfloat16)
    low = (rest - middle.astype(jnp.float32)).astype(jnp.bfloat16)
    return high, middle, low


def note_ids(ids, count, upright, across):
    slots = ids.shape[0]
    for s in range(slots):
        one = jnp.full((1, LANES), jnp.where(s < count, ids[s], -1), jnp.int32)
        upright[pl.ds(s, 1), :] = one
        upright[pl.ds(slots + s, 1), :] = one
    across[...] = upright[...].T


def merged(values, ids, count, upright, across, out):
    slots = values.shape[0]
    mine = upright[:slots, :]
    top = jnp.full((slots, LANES), NONE, jnp.float32)
    for s in range(slots):
        same = mine == jnp.where(s < count, ids[s], -1)
        top = jnp.maximum(top, jnp.where(same, values[pl.ds(s, 1), :], NONE))
    same = jnp.where(mine == across[:slots, :], 1.0, 0.0).astype(jnp.bfloat16)
    high, middle, _ = pieces(jnp.exp2(values[...] - top))
    mass = jnp.dot(same, jnp.concatenate([high, middle], axis=0), preferred_element_type=jnp.float32)
    out[:slots, :] = top + jnp.log2(mass)
    above = lax.broadcasted_iota(jnp.int32, (slots, LANES), 0)
    lane = lax.broadcasted_iota(jnp.int32, (slots, LANES), 1)
    earlier = above < jnp.where(lane < slots, lane, lane - slots)
    again = jnp.max(jnp.where(earlier & (mine == across[:slots, :]), 1.0, 0.0), axis=0, keepdims=True)
    named = jnp.where(again > 0.0, -1.0, across[:1, :].astype(jnp.float32))
    out[slots:, :] = jnp.broadcast_to(named, (out.shape[0] - slots, LANES))


def spread(parts, dense):
    peers = parts.shape[0]
    slots = LANES // 2
    block = lax.broadcasted_iota(jnp.int32, (LANES, LANES), 0).astype(jnp.float32)
    ones = jnp.ones((slots, LANES), jnp.bfloat16)
    none = jnp.zeros((slots, LANES), jnp.bfloat16)
    hits = jnp.concatenate([ones, none, none, none], axis=0)
    top = jnp.full((LANES, LANES), NONE, jnp.float32)
    for d in range(peers):
        pick = jnp.where(block == parts[d, slots : slots + 1, :], 1.0, 0.0).astype(jnp.bfloat16)
        high, middle, low = pieces(parts[d, :slots, :])
        cut = jnp.concatenate([high, middle, low, none], axis=0)
        both = jnp.dot(
            jnp.concatenate([pick, pick], axis=1),
            jnp.concatenate([cut, hits], axis=1),
            preferred_element_type=jnp.float32,
        )
        value = jnp.where(both[:, LANES:] > 0.5, both[:, :LANES], NONE)
        dense[d] = value
        top = jnp.maximum(top, value)
    total = jnp.zeros((LANES, LANES), jnp.float32)
    for d in range(peers):
        total = total + jnp.exp2(dense[d] - top)
    return jnp.maximum(top + jnp.log2(total), NONE)


def one_row_tile(part, tile):
    scores = ((part - tile) * UNIT).T
    top = jnp.max(scores, axis=0, keepdims=True)
    return top + jnp.log2(jnp.sum(jnp.exp2(scores - top), axis=0, keepdims=True))


def one_col_tile(part, tile):
    upright = jnp.broadcast_to(part, tile.shape).T
    scores = (upright - tile) * UNIT
    top = jnp.max(scores, axis=0, keepdims=True)
    return top + jnp.log2(jnp.sum(jnp.exp2(scores - top), axis=0, keepdims=True))


def fetch(cost_in, cost, sems):
    copies = []
    for k in range(cost.shape[0] // CHUNK):
        at = pl.ds(k * CHUNK, CHUNK)
        copies.append(pltpu.make_async_copy(cost_in.at[at], cost.at[at], sems.at[k]))
        copies[-1].start()
    return copies


def tiles(tile_lse, ids, chunks, cost, pot, values):
    for k, chunk in enumerate(chunks):
        chunk.wait()
        for s in range(k * CHUNK, (k + 1) * CHUNK):
            values[pl.ds(s, 1), :] = tile_lse(pot[pl.ds(ids[s], 1), :], cost[s])


def start_all(pairs, sems):
    copies = [pltpu.make_async_copy(src, dst, sems.at[k]) for k, (src, dst) in enumerate(pairs)]
    for copy in copies:
        copy.start()
    return copies


def source_side(rows, cols, chunks, small, count, cost, pot, values, upright, across, out):
    for copy in small:
        copy.wait()
    note_ids(rows, count, upright, across)
    tiles(one_row_tile, cols, chunks, cost, pot, values)
    merged(values, rows, count, upright, across, out)


def first_rows_kernel(
    rows_in, cols_in, cost_in, pot_in, count, out, cost, rows, cols, pot, sems, cost_sems, values, upright, across
):
    small = start_all(((cols_in, cols), (pot_in, pot), (rows_in, rows)), sems)
    chunks = fetch(cost_in, cost, cost_sems)
    source_side(rows, cols, chunks, small, count[0, 0], cost, pot, values, upright, across, out)


def rows_kernel(
    rows_in, cols_in, cost_in, count, mine, other, logmass, out, cost, rows, cols, pot, sems, cost_sems, values, upright, across
):
    small = start_all(((cols_in, cols), (rows_in, rows)), sems)
    chunks = fetch(cost_in, cost, cost_sems)
    pot[...] = EPS * logmass[...] - BACK * pair_lse2(mine[...], other[...])
    source_side(rows, cols, chunks, small, count[0, 0], cost, pot, values, upright, across, out)


def cols_kernel(
    rows_in, cols_in, cost_in, count, parts, logmass, pot, out, cost, rows, cols, spare, sems, cost_sems, values, upright, across, dense
):
    small = start_all(((rows_in, rows), (cols_in, cols)), sems)
    chunks = fetch(cost_in, cost, cost_sems)
    pot[...] = EPS * logmass[...] - BACK * spread(parts, dense)
    for copy in small:
        copy.wait()
    note_ids(cols, count[0, 0], upright, across)
    tiles(one_col_tile, rows, chunks, cost, pot, values)
    merged(values, cols, count[0, 0], upright, across, out)


def spread_kernel(parts, out, dense):
    out[...] = spread(parts, dense)


def pair_lse2(a, b):
    return jnp.maximum(a, b) + jnp.log2(1.0 + jnp.exp2(-jnp.abs(a - b)))


def call(kernel, name, anywhere, smem, vmem, outs, slots, extra):
    held = pl.BlockSpec(memory_space=pltpu.VMEM)
    specs = [pl.BlockSpec(memory_space=pl.ANY)] * len(anywhere)
    specs += [pl.BlockSpec(memory_space=pltpu.SMEM)] * len(smem) + [held] * len(vmem)
    single = len(outs) == 1
    scratch = []
    if anywhere:
        scratch = [
            pltpu.VMEM((slots, LANES, LANES), jnp.float32),
            pltpu.SMEM((slots,), jnp.int32),
            pltpu.SMEM((slots,), jnp.int32),
            pltpu.VMEM((LANES, LANES), jnp.float32),
            pltpu.SemaphoreType.DMA((3,)),
            pltpu.SemaphoreType.DMA((slots // CHUNK,)),
            pltpu.VMEM((slots, LANES), jnp.float32),
            pltpu.VMEM((LANES, LANES), jnp.int32),
            pltpu.VMEM((LANES, LANES), jnp.int32),
        ]
    return pl.pallas_call(
        kernel,
        name=name,
        out_shape=outs[0] if single else outs,
        in_specs=specs,
        out_specs=held if single else tuple(held for _ in outs),
        scratch_shapes=scratch + list(extra),
        compiler_params=pltpu.CompilerParams(vmem_limit_bytes=LIMIT),
    )(*[pltpu.with_memory_space_constraint(x, pltpu.HBM) for x in anywhere], *smem, *vmem)


def to_all(value, axes, peers):
    copies = jnp.broadcast_to(value[None], (peers, *value.shape))
    return lax.all_to_all(copies, axes, 0, 0, tiled=True)


def local(
    cost_tiles, tile_rows, tile_cols, tile_count, source_logmass, target_logmass, target_init
):
    cost = cost_tiles.reshape(cost_tiles.shape[2:])
    rows = tile_rows.reshape(-1)
    cols = tile_cols.reshape(-1)
    count = tile_count.reshape(1, 1)
    srcmass = source_logmass.reshape(-1, LANES)
    tgtmass = target_logmass.reshape(-1, LANES)
    ncol = lax.axis_size("col")
    nz = lax.axis_size("z")
    swap = [(0, 1), (1, 0)]
    slots = cost.shape[0]
    tiled = (rows, cols, cost)

    def f32(*shape):
        return jax.ShapeDtypeStruct(shape, jnp.float32)

    full, sent = f32(LANES, LANES), f32(slots + 8, LANES)
    for step in range(ITERS):
        if step == 0:
            listed = call(
                first_rows_kernel, "first_rows", (*tiled, target_init.reshape(-1, LANES)), (count,), (),
                (sent,), slots, (),
            )
        else:
            listed = call(
                rows_kernel, "rows_half", tiled, (count,), (mine, other, tgtmass), (sent,), slots, ()
            )
        parts = to_all(listed, "col", ncol).reshape(ncol, slots + 8, LANES)
        source, listed = call(
            cols_kernel, "cols_half", tiled, (count,), (parts, srcmass), (full, sent), slots,
            (pltpu.VMEM((ncol, LANES, LANES), jnp.float32),),
        )
        parts = to_all(listed, "z", nz).reshape(nz, slots + 8, LANES)
        mine = call(
            spread_kernel, "spread", (), (), (parts,), (full,), slots,
            (pltpu.VMEM((nz, LANES, LANES), jnp.float32),),
        )
        other = lax.ppermute(mine, "core", swap)
    target = EPS * tgtmass - BACK * pair_lse2(mine, other)
    return (source.reshape(-1), target.reshape(-1))


def solution(mesh):
    nrow, ncol = mesh.devices.shape
    cores = 2
    finer = Mesh(mesh.devices.reshape(nrow // cores, cores, ncol), ("z", "core", "col"))
    row = ("z", "core")
    return jax.shard_map(
        local,
        mesh=finer,
        in_specs=(
            P(row, "col", None, None, None),
            P(row, "col", None),
            P(row, "col", None),
            P(row, "col"),
            P(row),
            P("col"),
            P("col"),
        ),
        out_specs=(P(row), P("col")),
        check_vma=False,
    )
```

```python
import jax
import jax.numpy as jnp
import numpy as np
from jax import lax
from jax.experimental import pallas as pl
from jax.experimental.pallas import tpu as pltpu
from jax.sharding import Mesh
from jax.sharding import PartitionSpec as P

ITERS = 2
EPS = 0.1
LN2 = float(np.log(2.0))
UNIT = 1.0 / (EPS * LN2)
BACK = EPS * LN2
NONE = -1.0e30
LANES = 128
CHUNK = 8
LIMIT = 24 << 20


def pieces(x):
    high = x.astype(jnp.bfloat16)
    rest = x - high.astype(jnp.float32)
    middle = rest.astype(jnp.bfloat16)
    low = (rest - middle.astype(jnp.float32)).astype(jnp.bfloat16)
    return high, middle, low


def note_ids(ids, count, upright, same, named, scratch):
    slots = ids.shape[0]
    for s in range(slots):
        one = jnp.full((1, LANES), jnp.where(s < count, ids[s], -1), jnp.int32)
        scratch[pl.ds(s, 1), :] = one
        scratch[pl.ds(slots + s, 1), :] = one
    upright[...] = scratch[:slots, :]
    across = scratch[...].T[:slots, :]
    equal = upright[...] == across
    same[...] = jnp.where(equal, 1.0, 0.0)
    above = lax.broadcasted_iota(jnp.int32, (slots, LANES), 0)
    lane = lax.broadcasted_iota(jnp.int32, (slots, LANES), 1)
    earlier = above < jnp.where(lane < slots, lane, lane - slots)
    again = jnp.max(jnp.where(earlier & equal, 1.0, 0.0), axis=0, keepdims=True)
    once = jnp.where(again > 0.0, -1.0, across[:1, :].astype(jnp.float32))
    named[...] = jnp.broadcast_to(once, named.shape)


def gathered(pot, upright):
    block = lax.broadcasted_iota(jnp.int32, upright.shape, 1)
    pick = jnp.where(block == upright[...], 1.0, 0.0).astype(jnp.bfloat16)
    return jnp.dot(
        jnp.concatenate([pick, pick, pick], axis=1),
        jnp.concatenate(pieces(pot), axis=0),
        preferred_element_type=jnp.float32,
    )


def merged(values, upright, same, named, out):
    slots = values.shape[0]
    mine = upright[...]
    top = jnp.full((slots, LANES), NONE, jnp.float32)
    for s in range(slots):
        hit = mine == upright[pl.ds(s, 1), :]
        top = jnp.maximum(top, jnp.where(hit, values[pl.ds(s, 1), :], NONE))
    high, middle, _ = pieces(jnp.exp2(values[...] - top))
    mass = jnp.dot(
        same[...].astype(jnp.bfloat16),
        jnp.concatenate([high, middle], axis=0),
        preferred_element_type=jnp.float32,
    )
    out[:slots, :] = top + jnp.log2(mass)
    if out.shape[0] > slots:
        out[slots:, :] = named[...]


def spread(parts, names, dense):
    peers = parts.shape[0]
    slots = LANES // 2
    block = lax.broadcasted_iota(jnp.int32, (LANES, LANES), 0).astype(jnp.float32)
    ones = jnp.ones((slots, LANES), jnp.bfloat16)
    none = jnp.zeros((slots, LANES), jnp.bfloat16)
    hits = jnp.concatenate([ones, none, none, none], axis=0)
    top = jnp.full((LANES, LANES), NONE, jnp.float32)
    for d in range(peers):
        pick = jnp.where(block == names[d, slots : slots + 1, :], 1.0, 0.0).astype(jnp.bfloat16)
        high, middle, low = pieces(parts[d, :slots, :])
        cut = jnp.concatenate([high, middle, low, none], axis=0)
        both = jnp.dot(
            jnp.concatenate([pick, pick], axis=1),
            jnp.concatenate([cut, hits], axis=1),
            preferred_element_type=jnp.float32,
        )
        value = jnp.where(both[:, LANES:] > 0.5, both[:, :LANES], NONE)
        dense[d] = value
        top = jnp.maximum(top, value)
    total = jnp.zeros((LANES, LANES), jnp.float32)
    for d in range(peers):
        total = total + jnp.exp2(dense[d] - top)
    return jnp.maximum(top + jnp.log2(total), NONE)


def one_row_tile(part, tile):
    scores = ((part - tile) * UNIT).T
    top = jnp.max(scores, axis=0, keepdims=True)
    return top + jnp.log2(jnp.sum(jnp.exp2(scores - top), axis=0, keepdims=True))


def one_col_tile(part, tile):
    upright = jnp.broadcast_to(part, tile.shape).T
    scores = (upright - tile) * UNIT
    top = jnp.max(scores, axis=0, keepdims=True)
    return top + jnp.log2(jnp.sum(jnp.exp2(scores - top), axis=0, keepdims=True))


def tiles(tile_lse, cost, picked, values, chunks=None):
    for k in range(cost.shape[0] // CHUNK):
        if chunks:
            chunks[k].wait()
        for s in range(k * CHUNK, (k + 1) * CHUNK):
            values[pl.ds(s, 1), :] = tile_lse(picked[pl.ds(s, 1), :], cost[s])


def first_rows_kernel(
    rows_in, cols_in, cost_in, pot_in, count,
    out, cost, row_up, row_same, row_named, col_up, col_same, col_named,
    rows, cols, pot, sems, cost_sems, scratch, values, picked,
):
    small = []
    for k, (src, dst) in enumerate(((cols_in, cols), (rows_in, rows), (pot_in, pot))):
        small.append(pltpu.make_async_copy(src, dst, sems.at[k]))
        small[-1].start()
    chunks = []
    for k in range(cost.shape[0] // CHUNK):
        at = pl.ds(k * CHUNK, CHUNK)
        chunks.append(pltpu.make_async_copy(cost_in.at[at], cost.at[at], cost_sems.at[k]))
        chunks[-1].start()
    small[0].wait()
    note_ids(cols, count[0, 0], col_up, col_same, col_named, scratch)
    small[1].wait()
    note_ids(rows, count[0, 0], row_up, row_same, row_named, scratch)
    small[2].wait()
    picked[...] = gathered(pot[...], col_up)
    tiles(one_row_tile, cost, picked, values, chunks)
    merged(values, row_up, row_same, row_named, out)


def rows_kernel(mine, other, logmass, cost, row_up, row_same, row_named, col_up, out, values, picked):
    pot = EPS * logmass[...] - BACK * pair_lse2(mine[...], other[...])
    picked[...] = gathered(pot, col_up)
    tiles(one_row_tile, cost, picked, values)
    merged(values, row_up, row_same, row_named, out)


def cols_kernel(
    parts, names, logmass, cost, row_up, col_up, col_same, col_named, pot, out, values, picked, dense
):
    pot[...] = EPS * logmass[...] - BACK * spread(parts, names, dense)
    picked[...] = gathered(pot[...], row_up)
    tiles(one_col_tile, cost, picked, values)
    merged(values, col_up, col_same, col_named, out)


def spread_kernel(parts, names, out, dense):
    out[...] = spread(parts, names, dense)


def pair_lse2(a, b):
    return jnp.maximum(a, b) + jnp.log2(1.0 + jnp.exp2(-jnp.abs(a - b)))


def call(kernel, name, operands, specs, outs, scratch):
    held = pl.BlockSpec(memory_space=pltpu.VMEM)
    single = len(outs) == 1
    return pl.pallas_call(
        kernel,
        name=name,
        out_shape=outs[0] if single else outs,
        in_specs=[held] * len(operands) if specs is None else specs,
        out_specs=held if single else tuple(held for _ in outs),
        scratch_shapes=scratch,
        compiler_params=pltpu.CompilerParams(vmem_limit_bytes=LIMIT),
    )(*operands)


def to_all(value, axes, peers):
    copies = jnp.broadcast_to(value[None], (peers, *value.shape))
    return lax.all_to_all(copies, axes, 0, 0, tiled=True)


def local(
    cost_tiles, tile_rows, tile_cols, tile_count, source_logmass, target_logmass, target_init
):
    cost = cost_tiles.reshape(cost_tiles.shape[2:])
    rows = tile_rows.reshape(-1)
    cols = tile_cols.reshape(-1)
    count = tile_count.reshape(1, 1)
    srcmass = source_logmass.reshape(-1, LANES)
    tgtmass = target_logmass.reshape(-1, LANES)
    ncol = lax.axis_size("col")
    nz = lax.axis_size("z")
    swap = [(0, 1), (1, 0)]
    slots = cost.shape[0]

    def f32(*shape):
        return pltpu.VMEM(shape, jnp.float32)

    def keep(x):
        return pltpu.with_memory_space_constraint(x, pltpu.VMEM)

    def far(x):
        return pltpu.with_memory_space_constraint(x, pltpu.HBM)

    full, named, values = f32(LANES, LANES), f32(8, LANES), f32(slots, LANES)
    ids = (pltpu.VMEM((slots, LANES), jnp.int32), values, named)
    anywhere = pl.BlockSpec(memory_space=pl.ANY)
    col_names = row_names = None
    for step in range(ITERS):
        sent = f32(slots + 8, LANES) if step == 0 else f32(slots, LANES)
        if step == 0:
            listed, *kept = call(
                first_rows_kernel, "first_rows",
                (far(rows), far(cols), far(cost), far(target_init.reshape(-1, LANES)), count),
                [anywhere] * 4 + [pl.BlockSpec(memory_space=pltpu.SMEM)],
                (sent, f32(*cost.shape), *ids, *ids),
                (
                    pltpu.SMEM((slots,), jnp.int32),
                    pltpu.SMEM((slots,), jnp.int32),
                    full,
                    pltpu.SemaphoreType.DMA((3,)),
                    pltpu.SemaphoreType.DMA((slots // CHUNK,)),
                    pltpu.VMEM((LANES, LANES), jnp.int32),
                    values,
                    values,
                ),
            )
            tiles_held, row_up, row_same, row_named, col_up, col_same, col_named = (keep(x) for x in kept)
        else:
            listed = call(
                rows_kernel, "rows_half",
                (mine, other, tgtmass, tiles_held, row_up, row_same, row_named, col_up),
                None, (sent,), (values, values),
            )
        parts = to_all(listed, "col", ncol).reshape(ncol, -1, LANES)
        col_names = parts if step == 0 else col_names
        source, listed = call(
            cols_kernel, "cols_half",
            (parts, col_names, srcmass, tiles_held, row_up, col_up, col_same, col_named),
            None, (jax.ShapeDtypeStruct((LANES, LANES), jnp.float32), sent),
            (values, values, f32(ncol, LANES, LANES)),
        )
        parts = to_all(listed, "z", nz).reshape(nz, -1, LANES)
        row_names = parts if step == 0 else row_names
        mine = call(
            spread_kernel, "spread", (parts, row_names), None, (full,), (f32(nz, LANES, LANES),)
        )
        other = lax.ppermute(mine, "core", swap)
    target = EPS * tgtmass - BACK * pair_lse2(mine, other)
    return (source.reshape(-1), target.reshape(-1))


def solution(mesh):
    nrow, ncol = mesh.devices.shape
    cores = 2
    finer = Mesh(mesh.devices.reshape(nrow // cores, cores, ncol), ("z", "core", "col"))
    row = ("z", "core")
    return jax.shard_map(
        local,
        mesh=finer,
        in_specs=(
            P(row, "col", None, None, None),
            P(row, "col", None),
            P(row, "col", None),
            P(row, "col"),
            P(row),
            P("col"),
            P("col"),
        ),
        out_specs=(P(row), P("col")),
        check_vma=False,
    )
```

```python
import jax
import jax.numpy as jnp
import numpy as np
from jax import lax
from jax.experimental import pallas as pl
from jax.experimental.pallas import tpu as pltpu
from jax.sharding import Mesh
from jax.sharding import PartitionSpec as P

ITERS = 2
EPS = 0.1
LN2 = float(np.log(2.0))
UNIT = 1.0 / (EPS * LN2)
BACK = EPS * LN2
NONE = -1.0e30
LANES = 128
SLOTS = 64
RING = 4
CHUNK = 16
AHEAD = 2
LIMIT = 24 << 20


def pieces(x):
    high = x.astype(jnp.bfloat16)
    rest = x - high.astype(jnp.float32)
    middle = rest.astype(jnp.bfloat16)
    low = (rest - middle.astype(jnp.float32)).astype(jnp.bfloat16)
    return high, middle, low


def note_ids(ids, count, upright, same, named, scratch):
    slots = ids.shape[0]
    for s in range(slots):
        one = jnp.full((1, LANES), jnp.where(s < count, ids[s], -1), jnp.int32)
        scratch[pl.ds(s, 1), :] = one
        scratch[pl.ds(slots + s, 1), :] = one
    upright[...] = scratch[:slots, :]
    across = scratch[...].T[:slots, :]
    equal = upright[...] == across
    same[...] = jnp.where(equal, 1.0, 0.0)
    above = lax.broadcasted_iota(jnp.int32, (slots, LANES), 0)
    lane = lax.broadcasted_iota(jnp.int32, (slots, LANES), 1)
    earlier = above < jnp.where(lane < slots, lane, lane - slots)
    again = jnp.max(jnp.where(earlier & equal, 1.0, 0.0), axis=0, keepdims=True)
    once = jnp.where(again > 0.0, -1.0, across[:1, :].astype(jnp.float32))
    named[...] = jnp.broadcast_to(once, named.shape)


def gathered(pot, upright):
    block = lax.broadcasted_iota(jnp.int32, upright.shape, 1)
    pick = jnp.where(block == upright[...], 1.0, 0.0).astype(jnp.bfloat16)
    return jnp.dot(
        jnp.concatenate([pick, pick, pick], axis=1),
        jnp.concatenate(pieces(pot), axis=0),
        preferred_element_type=jnp.float32,
    )


def merged(values, upright, same, named, out):
    slots = values.shape[0]
    mine = upright[...]
    values[...] = jnp.where(mine >= 0, values[...], 0.0)
    top = jnp.full((slots, LANES), NONE, jnp.float32)
    for s in range(slots):
        hit = mine == upright[pl.ds(s, 1), :]
        top = jnp.maximum(top, jnp.where(hit, values[pl.ds(s, 1), :], NONE))
    high, middle, _ = pieces(jnp.exp2(values[...] - top))
    mass = jnp.dot(
        same[...].astype(jnp.bfloat16),
        jnp.concatenate([high, middle], axis=0),
        preferred_element_type=jnp.float32,
    )
    out[:slots, :] = top + jnp.log2(mass)
    if out.shape[0] > slots:
        out[slots:, :] = named[...]


def placed(rows, ids):
    block = lax.broadcasted_iota(jnp.int32, (LANES, LANES), 0).astype(jnp.float32)
    ones = jnp.ones((SLOTS, LANES), jnp.bfloat16)
    none = jnp.zeros((SLOTS, LANES), jnp.bfloat16)
    pick = jnp.where(block == ids, 1.0, 0.0).astype(jnp.bfloat16)
    both = jnp.dot(
        jnp.concatenate([pick, pick], axis=1),
        jnp.concatenate(
            [jnp.concatenate([*pieces(rows), none], axis=0), jnp.concatenate([ones, none, none, none], axis=0)],
            axis=1,
        ),
        preferred_element_type=jnp.float32,
    )
    return jnp.where(both[:, LANES:] > 0.5, both[:, :LANES], NONE)


def spread(parts, names, dense):
    top = jnp.full((LANES, LANES), NONE, jnp.float32)
    for d in range(parts.shape[0]):
        value = placed(parts[d, :SLOTS, :], names[d, SLOTS : SLOTS + 1, :])
        dense[d] = value
        top = jnp.maximum(top, value)
    total = jnp.zeros((LANES, LANES), jnp.float32)
    for d in range(parts.shape[0]):
        total = total + jnp.exp2(dense[d] - top)
    return jnp.maximum(top + jnp.log2(total), NONE)


def one_row_tile(part, tile):
    scores = ((part - tile) * UNIT).T
    top = jnp.max(scores, axis=0, keepdims=True)
    return top + jnp.log2(jnp.sum(jnp.exp2(scores - top), axis=0, keepdims=True))


def one_col_tile(part, tile):
    upright = jnp.broadcast_to(part, tile.shape).T
    scores = (upright - tile) * UNIT
    top = jnp.max(scores, axis=0, keepdims=True)
    return top + jnp.log2(jnp.sum(jnp.exp2(scores - top), axis=0, keepdims=True))


def tiles(tile_lse, cost, picked, values):
    for s in range(cost.shape[0]):
        values[pl.ds(s, 1), :] = tile_lse(picked[pl.ds(s, 1), :], cost[s])


def first_rows_kernel(
    rows_in, cols_in, cost_in, pot_in, count_in,
    out, cost, row_up, row_same, row_named, col_up, col_same, col_named,
    rows, cols, pot, sems, cost_sems, scratch, values, picked,
):
    count = count_in[0, 0]
    small = []
    for k, (src, dst) in enumerate(((cols_in, cols), (rows_in, rows), (pot_in, pot))):
        small.append(pltpu.make_async_copy(src, dst, sems.at[k]))
        small[-1].start()
    chunks = []
    for k in range(cost.shape[0] // CHUNK):
        at = pl.ds(k * CHUNK, CHUNK)
        chunks.append(pltpu.make_async_copy(cost_in.at[at], cost.at[at], cost_sems.at[k]))
        if k < AHEAD:
            pl.when(count > k * CHUNK)(chunks[k].start)
    values[...] = jnp.zeros(values.shape, jnp.float32)
    for copy in small:
        copy.wait()
    note_ids(cols, count, col_up, col_same, col_named, scratch)
    picked[...] = gathered(pot[...], col_up)
    note_ids(rows, count, row_up, row_same, row_named, scratch)
    for k, chunk in enumerate(chunks):

        @pl.when(count > k * CHUNK)
        def _():
            chunk.wait()
            if k + AHEAD < len(chunks):
                pl.when(count > (k + AHEAD) * CHUNK)(chunks[k + AHEAD].start)
            for s in range(k * CHUNK, (k + 1) * CHUNK):
                values[pl.ds(s, 1), :] = one_row_tile(picked[pl.ds(s, 1), :], cost[s])

    merged(values, row_up, row_same, row_named, out)


def rows_kernel(mine, other, logmass, cost, row_up, row_same, row_named, col_up, out, values, picked):
    pot = EPS * logmass[...] - BACK * pair_lse2(mine[...], other[...])
    picked[...] = gathered(pot, col_up)
    tiles(one_row_tile, cost, picked, values)
    merged(values, row_up, row_same, row_named, out)


def cols_kernel(
    one, two, three, four, logmass, cost, row_up, col_up, col_same, col_named, pot, out, values, picked
):
    pot[...] = EPS * logmass[...] - BACK * ring_lse2([x[...] for x in (one, two, three, four)])
    picked[...] = gathered(pot[...], row_up)
    tiles(one_col_tile, cost, picked, values)
    merged(values, col_up, col_same, col_named, out)


def ring_lse2(parts):
    top = jnp.maximum(jnp.maximum(parts[0], parts[2]), jnp.maximum(parts[1], parts[3]))
    own, after, across, before = (jnp.exp2(part - top) for part in parts)
    return jnp.maximum(top + jnp.log2((own + across) + (after + before)), NONE)


def ring_kernel(*refs):
    parts, names, out = refs[:4], refs[4:8], refs[8]
    out[...] = ring_lse2([placed(part[:SLOTS, :], name[SLOTS : SLOTS + 1, :]) for part, name in zip(parts, names)])


def spread_kernel(parts, names, out, dense):
    out[...] = spread(parts, names, dense)


def pair_lse2(a, b):
    return jnp.maximum(a, b) + jnp.log2(1.0 + jnp.exp2(-jnp.abs(a - b)))


def call(kernel, name, operands, specs, outs, scratch):
    held = pl.BlockSpec(memory_space=pltpu.VMEM)
    single = len(outs) == 1
    return pl.pallas_call(
        kernel,
        name=name,
        out_shape=outs[0] if single else outs,
        in_specs=[held] * len(operands) if specs is None else specs,
        out_specs=held if single else tuple(held for _ in outs),
        scratch_shapes=scratch,
        compiler_params=pltpu.CompilerParams(vmem_limit_bytes=LIMIT),
    )(*operands)


def ring(value, nz, stage):
    got = {0: value}
    for hop in (2, 1, 3):
        pairs = []
        for z in range(nz):
            for core in range(2):
                for x in range(RING):
                    for y in range(RING):
                        along_x = core == stage
                        to = ((x + hop) % RING, y) if along_x else (x, (y + hop) % RING)
                        row = (z * 2 + core) * RING
                        pairs.append(((row + x) * RING + y, (row + to[0]) * RING + to[1]))
        got[hop] = lax.ppermute(value, ("z", "core", "col"), pairs)
    return [got[hop] for hop in range(RING)]


def to_all(value, axes, peers):
    copies = jnp.broadcast_to(value[None], (peers, *value.shape))
    return lax.all_to_all(copies, axes, 0, 0, tiled=True)


def local(
    cost_tiles, tile_rows, tile_cols, tile_count, source_logmass, target_logmass, target_init
):
    cost = cost_tiles.reshape(cost_tiles.shape[2:])
    rows = tile_rows.reshape(-1)
    cols = tile_cols.reshape(-1)
    count = tile_count.reshape(1, 1)
    srcmass = source_logmass.reshape(-1, LANES)
    tgtmass = target_logmass.reshape(-1, LANES)
    nz = lax.axis_size("z")
    swap = [(0, 1), (1, 0)]
    slots = cost.shape[0]

    def f32(*shape):
        return pltpu.VMEM(shape, jnp.float32)

    def keep(x):
        return pltpu.with_memory_space_constraint(x, pltpu.VMEM)

    def far(x):
        return pltpu.with_memory_space_constraint(x, pltpu.HBM)

    full, named, values = f32(LANES, LANES), f32(8, LANES), f32(slots, LANES)
    ids = (pltpu.VMEM((slots, LANES), jnp.int32), values, named)
    anywhere = pl.BlockSpec(memory_space=pl.ANY)
    col_names = row_names = None
    for step in range(ITERS):
        sent = f32(slots + 8, LANES) if step == 0 else f32(slots, LANES)
        if step == 0:
            listed, *kept = call(
                first_rows_kernel, "first_rows",
                (far(rows), far(cols), far(cost), far(target_init.reshape(-1, LANES)), count),
                [anywhere] * 4 + [pl.BlockSpec(memory_space=pltpu.SMEM)],
                (sent, f32(*cost.shape), *ids, *ids),
                (
                    pltpu.SMEM((slots,), jnp.int32),
                    pltpu.SMEM((slots,), jnp.int32),
                    full,
                    pltpu.SemaphoreType.DMA((3,)),
                    pltpu.SemaphoreType.DMA((slots // CHUNK,)),
                    pltpu.VMEM((LANES, LANES), jnp.int32),
                    values,
                    values,
                ),
            )
            tiles_held, row_up, row_same, row_named, col_up, col_same, col_named = (keep(x) for x in kept)
        else:
            listed = call(
                rows_kernel, "rows_half",
                (mine, other, tgtmass, tiles_held, row_up, row_same, row_named, col_up),
                None, (sent,), (values, values),
            )
        parts = ring(listed, nz, 0)
        col_names = parts if step == 0 else col_names
        part = call(ring_kernel, "ring", (*parts, *col_names), None, (full,), ())
        source, listed = call(
            cols_kernel, "cols_half",
            (*ring(part, nz, 1), srcmass, tiles_held, row_up, col_up, col_same, col_named),
            None, (jax.ShapeDtypeStruct((LANES, LANES), jnp.float32), sent),
            (values, values),
        )
        parts = to_all(listed, "z", nz).reshape(nz, -1, LANES)
        row_names = parts if step == 0 else row_names
        mine = call(
            spread_kernel, "spread", (parts, row_names), None, (full,), (f32(nz, LANES, LANES),)
        )
        other = lax.ppermute(mine, "core", swap)
    target = EPS * tgtmass - BACK * pair_lse2(mine, other)
    return (source.reshape(-1), target.reshape(-1))


def solution(mesh):
    nrow, ncol = mesh.devices.shape
    cores = 2
    finer = Mesh(mesh.devices.reshape(nrow // cores, cores, ncol), ("z", "core", "col"))
    row = ("z", "core")
    return jax.shard_map(
        local,
        mesh=finer,
        in_specs=(
            P(row, "col", None, None, None),
            P(row, "col", None),
            P(row, "col", None),
            P(row, "col"),
            P(row),
            P("col"),
            P("col"),
        ),
        out_specs=(P(row), P("col")),
        check_vma=False,
    )
```

```python
import jax
import jax.numpy as jnp
import numpy as np
from jax import lax
from jax.experimental import pallas as pl
from jax.experimental.pallas import tpu as pltpu
from jax.sharding import Mesh
from jax.sharding import PartitionSpec as P

ITERS = 2
EPS = 0.1
LN2 = float(np.log(2.0))
UNIT = 1.0 / (EPS * LN2)
BACK = EPS * LN2
NONE = -1.0e30
LANES = 128
SLOTS = 64
RING = 4
CHUNK = 16
AHEAD = 2
LIMIT = 24 << 20


def pieces(x):
    high = x.astype(jnp.bfloat16)
    rest = x - high.astype(jnp.float32)
    middle = rest.astype(jnp.bfloat16)
    low = (rest - middle.astype(jnp.float32)).astype(jnp.bfloat16)
    return high, middle, low


def note_ids(ids, count, upright, same, named, scratch):
    slots = ids.shape[0]
    for s in range(slots):
        one = jnp.full((1, LANES), jnp.where(s < count, ids[s], -1), jnp.int32)
        scratch[pl.ds(s, 1), :] = one
        scratch[pl.ds(slots + s, 1), :] = one
    upright[...] = scratch[:slots, :]
    across = scratch[...].T[:slots, :]
    equal = upright[...] == across
    same[...] = jnp.where(equal, 1.0, 0.0)
    above = lax.broadcasted_iota(jnp.int32, (slots, LANES), 0)
    lane = lax.broadcasted_iota(jnp.int32, (slots, LANES), 1)
    earlier = above < jnp.where(lane < slots, lane, lane - slots)
    again = jnp.max(jnp.where(earlier & equal, 1.0, 0.0), axis=0, keepdims=True)
    once = jnp.where(again > 0.0, -1.0, across[:1, :].astype(jnp.float32))
    named[...] = jnp.broadcast_to(once, named.shape)


def gathered(pot, upright):
    block = lax.broadcasted_iota(jnp.int32, upright.shape, 1)
    pick = jnp.where(block == upright[...], 1.0, 0.0).astype(jnp.bfloat16)
    return jnp.dot(
        jnp.concatenate([pick, pick, pick], axis=1),
        jnp.concatenate(pieces(pot), axis=0),
        preferred_element_type=jnp.float32,
    )


def merged(values, upright, same, out):
    slots = values.shape[0]
    mine = upright[...]
    values[...] = jnp.where(mine >= 0, values[...], 0.0)
    top = jnp.full((slots, LANES), NONE, jnp.float32)
    for s in range(slots):
        hit = mine == upright[pl.ds(s, 1), :]
        top = jnp.maximum(top, jnp.where(hit, values[pl.ds(s, 1), :], NONE))
    high, middle, _ = pieces(jnp.exp2(values[...] - top))
    mass = jnp.dot(
        same[...].astype(jnp.bfloat16),
        jnp.concatenate([high, middle], axis=0),
        preferred_element_type=jnp.float32,
    )
    out[:slots, :] = top + jnp.log2(mass)


def placed(rows, ids):
    block = lax.broadcasted_iota(jnp.int32, (LANES, LANES), 0).astype(jnp.float32)
    ones = jnp.ones((SLOTS, LANES), jnp.bfloat16)
    none = jnp.zeros((SLOTS, LANES), jnp.bfloat16)
    pick = jnp.where(block == ids, 1.0, 0.0).astype(jnp.bfloat16)
    both = jnp.dot(
        jnp.concatenate([pick, pick], axis=1),
        jnp.concatenate(
            [jnp.concatenate([*pieces(rows), none], axis=0), jnp.concatenate([ones, none, none, none], axis=0)],
            axis=1,
        ),
        preferred_element_type=jnp.float32,
    )
    return jnp.where(both[:, LANES:] > 0.5, both[:, :LANES], NONE)


def spread(parts, names, dense):
    top = jnp.full((LANES, LANES), NONE, jnp.float32)
    for d in range(parts.shape[0]):
        value = placed(parts[d, :SLOTS, :], names[d, SLOTS : SLOTS + 1, :])
        dense[d] = value
        top = jnp.maximum(top, value)
    total = jnp.zeros((LANES, LANES), jnp.float32)
    for d in range(parts.shape[0]):
        total = total + jnp.exp2(dense[d] - top)
    return jnp.maximum(top + jnp.log2(total), NONE)


def add_names(named, out):
    if out.shape[0] > SLOTS:
        out[SLOTS:, :] = named[...]


def one_row_tile(part, tile):
    scores = (part - tile).T
    top = jnp.max(scores, axis=0, keepdims=True)
    return top + jnp.log2(jnp.sum(jnp.exp2(scores - top), axis=0, keepdims=True))


def one_col_tile(part, tile):
    upright = jnp.broadcast_to(part, tile.shape).T
    scores = upright - tile
    top = jnp.max(scores, axis=0, keepdims=True)
    return top + jnp.log2(jnp.sum(jnp.exp2(scores - top), axis=0, keepdims=True))


def tiles(tile_lse, cost, picked, values):
    for s in range(cost.shape[0]):
        values[pl.ds(s, 1), :] = tile_lse(picked[pl.ds(s, 1), :], cost[s])


def first_rows_kernel(
    rows_in, cols_in, cost_in, pot_in, count_in,
    out, cost, row_up, row_same, row_named, col_up, col_same, col_named,
    landing, rows, cols, pot, sems, cost_sems, scratch, values, picked,
):
    count = count_in[0, 0]
    small = []
    for k, (src, dst) in enumerate(((cols_in, cols), (rows_in, rows), (pot_in, pot))):
        small.append(pltpu.make_async_copy(src, dst, sems.at[k]))
        small[-1].start()
    chunks = []
    for k in range(cost.shape[0] // CHUNK):
        at = pl.ds(k * CHUNK, CHUNK)
        chunks.append(pltpu.make_async_copy(cost_in.at[at], landing.at[at], cost_sems.at[k]))
        if k < AHEAD:
            pl.when(count > k * CHUNK)(chunks[k].start)
    values[...] = jnp.zeros(values.shape, jnp.float32)
    for copy in small:
        copy.wait()
    note_ids(cols, count, col_up, col_same, col_named, scratch)
    picked[...] = gathered(UNIT * pot[...], col_up)
    note_ids(rows, count, row_up, row_same, row_named, scratch)
    add_names(row_named, out)
    for k, chunk in enumerate(chunks):

        @pl.when(count > k * CHUNK)
        def _():
            chunk.wait()
            if k + AHEAD < len(chunks):
                pl.when(count > (k + AHEAD) * CHUNK)(chunks[k + AHEAD].start)
            for s in range(k * CHUNK, (k + 1) * CHUNK):
                tile = UNIT * landing[s]
                cost[s] = tile
                values[pl.ds(s, 1), :] = one_row_tile(picked[pl.ds(s, 1), :], tile)

    merged(values, row_up, row_same, out)


def rows_kernel(mine, other, logmass, cost, row_up, row_same, row_named, col_up, out, values, picked):
    add_names(row_named, out)
    pot = EPS * logmass[...] - BACK * pair_lse2(mine[...], other[...])
    picked[...] = gathered(UNIT * pot, col_up)
    tiles(one_row_tile, cost, picked, values)
    merged(values, row_up, row_same, out)


def cols_kernel(
    one, two, three, four, logmass, cost, row_up, col_up, col_same, col_named, pot, out, values, picked
):
    add_names(col_named, out)
    pot[...] = EPS * logmass[...] - BACK * ring_lse2([x[...] for x in (one, two, three, four)])
    picked[...] = gathered(UNIT * pot[...], row_up)
    tiles(one_col_tile, cost, picked, values)
    merged(values, col_up, col_same, out)


def ring_lse2(parts):
    top = jnp.maximum(jnp.maximum(parts[0], parts[2]), jnp.maximum(parts[1], parts[3]))
    own, after, across, before = (jnp.exp2(part - top) for part in parts)
    return jnp.maximum(top + jnp.log2((own + across) + (after + before)), NONE)


def ring_kernel(*refs):
    parts, names, out = refs[:4], refs[4:8], refs[8]
    out[...] = ring_lse2([placed(part[:SLOTS, :], name[SLOTS : SLOTS + 1, :]) for part, name in zip(parts, names)])


def spread_kernel(parts, names, out, dense):
    out[...] = spread(parts, names, dense)


def pair_lse2(a, b):
    return jnp.maximum(a, b) + jnp.log2(1.0 + jnp.exp2(-jnp.abs(a - b)))


def call(kernel, name, operands, specs, outs, scratch):
    held = pl.BlockSpec(memory_space=pltpu.VMEM)
    single = len(outs) == 1
    return pl.pallas_call(
        kernel,
        name=name,
        out_shape=outs[0] if single else outs,
        in_specs=[held] * len(operands) if specs is None else specs,
        out_specs=held if single else tuple(held for _ in outs),
        scratch_shapes=scratch,
        compiler_params=pltpu.CompilerParams(vmem_limit_bytes=LIMIT),
    )(*operands)


def ring(value, nz, stage):
    got = {0: value}
    for hop in (2, 1, 3):
        pairs = []
        for z in range(nz):
            for core in range(2):
                for x in range(RING):
                    for y in range(RING):
                        along_x = core == stage
                        to = ((x + hop) % RING, y) if along_x else (x, (y + hop) % RING)
                        row = (z * 2 + core) * RING
                        pairs.append(((row + x) * RING + y, (row + to[0]) * RING + to[1]))
        got[hop] = lax.ppermute(value, ("z", "core", "col"), pairs)
    return [got[hop] for hop in range(RING)]


def to_all(value, axes, peers):
    copies = jnp.broadcast_to(value[None], (peers, *value.shape))
    return lax.all_to_all(copies, axes, 0, 0, tiled=True)


def local(
    cost_tiles, tile_rows, tile_cols, tile_count, source_logmass, target_logmass, target_init
):
    cost = cost_tiles.reshape(cost_tiles.shape[2:])
    rows = tile_rows.reshape(-1)
    cols = tile_cols.reshape(-1)
    count = tile_count.reshape(1, 1)
    srcmass = source_logmass.reshape(-1, LANES)
    tgtmass = target_logmass.reshape(-1, LANES)
    nz = lax.axis_size("z")
    swap = [(0, 1), (1, 0)]
    slots = cost.shape[0]

    def f32(*shape):
        return pltpu.VMEM(shape, jnp.float32)

    def keep(x):
        return pltpu.with_memory_space_constraint(x, pltpu.VMEM)

    def far(x):
        return pltpu.with_memory_space_constraint(x, pltpu.HBM)

    full, named, values = f32(LANES, LANES), f32(8, LANES), f32(slots, LANES)
    ids = (pltpu.VMEM((slots, LANES), jnp.int32), values, named)
    anywhere = pl.BlockSpec(memory_space=pl.ANY)
    col_names = row_names = None
    for step in range(ITERS):
        sent = f32(slots + 8, LANES) if step == 0 else f32(slots, LANES)
        if step == 0:
            listed, *kept = call(
                first_rows_kernel, "first_rows",
                (far(rows), far(cols), far(cost), far(target_init.reshape(-1, LANES)), count),
                [anywhere] * 4 + [pl.BlockSpec(memory_space=pltpu.SMEM)],
                (sent, f32(*cost.shape), *ids, *ids),
                (
                    f32(*cost.shape),
                    pltpu.SMEM((slots,), jnp.int32),
                    pltpu.SMEM((slots,), jnp.int32),
                    full,
                    pltpu.SemaphoreType.DMA((3,)),
                    pltpu.SemaphoreType.DMA((slots // CHUNK,)),
                    pltpu.VMEM((LANES, LANES), jnp.int32),
                    values,
                    values,
                ),
            )
            tiles_held, row_up, row_same, row_named, col_up, col_same, col_named = (keep(x) for x in kept)
        else:
            listed = call(
                rows_kernel, "rows_half",
                (mine, other, tgtmass, tiles_held, row_up, row_same, row_named, col_up),
                None, (sent,), (values, values),
            )
        parts = ring(listed, nz, 0)
        col_names = parts if step == 0 else col_names
        part = call(ring_kernel, "ring", (*parts, *col_names), None, (full,), ())
        source, listed = call(
            cols_kernel, "cols_half",
            (*ring(part, nz, 1), srcmass, tiles_held, row_up, col_up, col_same, col_named),
            None, (jax.ShapeDtypeStruct((LANES, LANES), jnp.float32), sent),
            (values, values),
        )
        parts = to_all(listed, "z", nz).reshape(nz, -1, LANES)
        row_names = parts if step == 0 else row_names
        mine = call(
            spread_kernel, "spread", (parts, row_names), None, (full,), (f32(nz, LANES, LANES),)
        )
        other = lax.ppermute(mine, "core", swap)
    target = EPS * tgtmass - BACK * pair_lse2(mine, other)
    return (source.reshape(-1), target.reshape(-1))


def solution(mesh):
    nrow, ncol = mesh.devices.shape
    cores = 2
    finer = Mesh(mesh.devices.reshape(nrow // cores, cores, ncol), ("z", "core", "col"))
    row = ("z", "core")
    return jax.shard_map(
        local,
        mesh=finer,
        in_specs=(
            P(row, "col", None, None, None),
            P(row, "col", None),
            P(row, "col", None),
            P(row, "col"),
            P(row),
            P("col"),
            P("col"),
        ),
        out_specs=(P(row), P("col")),
        check_vma=False,
    )
```

```python
import jax
import jax.numpy as jnp
import numpy as np
from jax import lax
from jax.experimental import pallas as pl
from jax.experimental.pallas import tpu as pltpu
from jax.sharding import Mesh
from jax.sharding import PartitionSpec as P

ITERS = 2
EPS = 0.1
LN2 = float(np.log(2.0))
UNIT = 1.0 / (EPS * LN2)
BACK = EPS * LN2
NONE = -1.0e30
LANES = 128
SLOTS = 64
RING = 4
CHUNK = 16
AHEAD = 2
LIMIT = 24 << 20


def pieces(x):
    high = x.astype(jnp.bfloat16)
    rest = x - high.astype(jnp.float32)
    middle = rest.astype(jnp.bfloat16)
    low = (rest - middle.astype(jnp.float32)).astype(jnp.bfloat16)
    return high, middle, low


def note_ids(ids, count, upright, same, named, scratch):
    slots = ids.shape[0]
    for s in range(slots):
        one = jnp.full((1, LANES), jnp.where(s < count, ids[s], -1), jnp.int32)
        scratch[pl.ds(s, 1), :] = one
        scratch[pl.ds(slots + s, 1), :] = one
    upright[...] = scratch[:slots, :]
    across = scratch[...].T[:slots, :]
    equal = upright[...] == across
    same[...] = jnp.where(equal, 1.0, 0.0)
    above = lax.broadcasted_iota(jnp.int32, (slots, LANES), 0)
    lane = lax.broadcasted_iota(jnp.int32, (slots, LANES), 1)
    earlier = above < jnp.where(lane < slots, lane, lane - slots)
    again = jnp.max(jnp.where(earlier & equal, 1.0, 0.0), axis=0, keepdims=True)
    once = jnp.where(again > 0.0, -1.0, across[:1, :].astype(jnp.float32))
    named[...] = jnp.broadcast_to(once, named.shape)


def gathered(pot, upright):
    block = lax.broadcasted_iota(jnp.int32, upright.shape, 1)
    pick = jnp.where(block == upright[...], 1.0, 0.0).astype(jnp.bfloat16)
    return jnp.dot(
        jnp.concatenate([pick, pick, pick], axis=1),
        jnp.concatenate(pieces(pot), axis=0),
        preferred_element_type=jnp.float32,
    )


def merged(values, upright, same, out):
    slots = values.shape[0]
    mine = upright[...]
    values[...] = jnp.where(mine >= 0, values[...], 0.0)
    top = jnp.full((slots, LANES), NONE, jnp.float32)
    for s in range(slots):
        hit = mine == upright[pl.ds(s, 1), :]
        top = jnp.maximum(top, jnp.where(hit, values[pl.ds(s, 1), :], NONE))
    high, middle, _ = pieces(jnp.exp2(values[...] - top))
    mass = jnp.dot(
        same[...].astype(jnp.bfloat16),
        jnp.concatenate([high, middle], axis=0),
        preferred_element_type=jnp.float32,
    )
    out[:slots, :] = top + jnp.log2(mass)


def placed(rows, ids):
    block = lax.broadcasted_iota(jnp.int32, (LANES, LANES), 0).astype(jnp.float32)
    ones = jnp.ones((SLOTS, LANES), jnp.bfloat16)
    none = jnp.zeros((SLOTS, LANES), jnp.bfloat16)
    pick = jnp.where(block == ids, 1.0, 0.0).astype(jnp.bfloat16)
    both = jnp.dot(
        jnp.concatenate([pick, pick], axis=1),
        jnp.concatenate(
            [jnp.concatenate([*pieces(rows), none], axis=0), jnp.concatenate([ones, none, none, none], axis=0)],
            axis=1,
        ),
        preferred_element_type=jnp.float32,
    )
    return jnp.where(both[:, LANES:] > 0.5, both[:, :LANES], NONE)


def spread(parts, names, dense):
    top = jnp.full((LANES, LANES), NONE, jnp.float32)
    for d in range(parts.shape[0]):
        value = placed(parts[d, :SLOTS, :], names[d, SLOTS : SLOTS + 1, :])
        dense[d] = value
        top = jnp.maximum(top, value)
    total = jnp.zeros((LANES, LANES), jnp.float32)
    for d in range(parts.shape[0]):
        total = total + jnp.exp2(dense[d] - top)
    return jnp.maximum(top + jnp.log2(total), NONE)


def add_names(named, out):
    if out.shape[0] > SLOTS:
        out[SLOTS:, :] = named[...]


def one_row_tile(part, tile):
    scores = (part - tile).T
    top = jnp.max(scores, axis=0, keepdims=True)
    return top + jnp.log2(jnp.sum(jnp.exp2(scores - top), axis=0, keepdims=True))


def one_col_tile(part, tile):
    upright = jnp.broadcast_to(part, tile.shape).T
    scores = upright - tile
    top = jnp.max(scores, axis=0, keepdims=True)
    return top + jnp.log2(jnp.sum(jnp.exp2(scores - top), axis=0, keepdims=True))


def tiles(tile_lse, cost, picked, values):
    for s in range(cost.shape[0]):
        values[pl.ds(s, 1), :] = tile_lse(picked[pl.ds(s, 1), :], cost[s])


def first_rows_kernel(
    rows_in, cols_in, cost_in, pot_in, count_in,
    out, cost, row_up, row_same, row_named, col_up, col_same, col_named,
    landing, rows, cols, pot, sems, cost_sems, scratch, values, picked,
):
    count = count_in[0, 0]
    small = []
    for k, (src, dst) in enumerate(((cols_in, cols), (rows_in, rows), (pot_in, pot))):
        small.append(pltpu.make_async_copy(src, dst, sems.at[k]))
        small[-1].start()
    chunks = []
    for k in range(cost.shape[0] // CHUNK):
        at = pl.ds(k * CHUNK, CHUNK)
        chunks.append(pltpu.make_async_copy(cost_in.at[at], landing.at[at], cost_sems.at[k]))
        if k < AHEAD:
            pl.when(count > k * CHUNK)(chunks[k].start)
    values[...] = jnp.zeros(values.shape, jnp.float32)
    for copy in small:
        copy.wait()
    note_ids(cols, count, col_up, col_same, col_named, scratch)
    picked[...] = gathered(UNIT * pot[...], col_up)
    note_ids(rows, count, row_up, row_same, row_named, scratch)
    add_names(row_named, out)
    for k, chunk in enumerate(chunks):

        @pl.when(count > k * CHUNK)
        def _():
            chunk.wait()
            if k + AHEAD < len(chunks):
                pl.when(count > (k + AHEAD) * CHUNK)(chunks[k + AHEAD].start)
            for s in range(k * CHUNK, (k + 1) * CHUNK):
                tile = UNIT * landing[s]
                cost[s] = tile
                values[pl.ds(s, 1), :] = one_row_tile(picked[pl.ds(s, 1), :], tile)

    merged(values, row_up, row_same, out)


def rows_kernel(mine, other, logmass, cost, row_up, row_same, row_named, col_up, out, values, picked):
    add_names(row_named, out)
    pot = EPS * logmass[...] - BACK * pair_lse2(mine[...], other[...])
    picked[...] = gathered(UNIT * pot, col_up)
    tiles(one_row_tile, cost, picked, values)
    merged(values, row_up, row_same, out)


def cols_kernel(
    one, two, three, four, logmass, cost, row_up, col_up, col_same, col_named, pot, out, values, picked
):
    add_names(col_named, out)
    pot[...] = EPS * logmass[...] - BACK * ring_lse2([x[...] for x in (one, two, three, four)])
    picked[...] = gathered(UNIT * pot[...], row_up)
    tiles(one_col_tile, cost, picked, values)
    merged(values, col_up, col_same, out)


def ring_lse2(parts):
    top = jnp.maximum(jnp.maximum(parts[0], parts[2]), jnp.maximum(parts[1], parts[3]))
    own, after, across, before = (jnp.exp2(part - top) for part in parts)
    return jnp.maximum(top + jnp.log2((own + across) + (after + before)), NONE)


def ring_kernel(*refs):
    parts, names, out = refs[:4], refs[4:8], refs[8]
    out[...] = ring_lse2([placed(part[:SLOTS, :], name[SLOTS : SLOTS + 1, :]) for part, name in zip(parts, names)])


def spread_kernel(parts, names, out, dense):
    out[...] = spread(parts, names, dense)


def pair_lse2(a, b):
    return jnp.maximum(a, b) + jnp.log2(1.0 + jnp.exp2(-jnp.abs(a - b)))


def call(kernel, name, operands, specs, outs, scratch):
    held = pl.BlockSpec(memory_space=pltpu.VMEM)
    single = len(outs) == 1
    return pl.pallas_call(
        kernel,
        name=name,
        out_shape=outs[0] if single else outs,
        in_specs=[held] * len(operands) if specs is None else specs,
        out_specs=held if single else tuple(held for _ in outs),
        scratch_shapes=scratch,
        compiler_params=pltpu.CompilerParams(vmem_limit_bytes=LIMIT),
    )(*operands)


def exchange(value, nz, routes):
    got = [value]
    for route in routes:
        pairs = []
        for z in range(nz):
            for core in range(2):
                for x in range(RING):
                    for y in range(RING):
                        to = route(z, core, x, y)
                        here = ((z * 2 + core) * RING + x) * RING + y
                        pairs.append((here, ((to[0] * 2 + to[1]) * RING + to[2]) * RING + to[3]))
        got.append(lax.ppermute(value, ("z", "core", "col"), pairs))
    return got


def ring_routes(stage):
    def route(hop):
        def to(z, core, x, y):
            if core == stage:
                return z, core, (x + hop) % RING, y
            return z, core, x, (y + hop) % RING

        return to

    return [route(hop) for hop in (1, 2, 3)]


def pair_routes():
    return [
        lambda z, core, x, y: (z ^ 1, core, x, y),
        lambda z, core, x, y: (z, 1 - core, x, y),
        lambda z, core, x, y: (z ^ 1, 1 - core, x, y),
    ]


def line_routes(nz):
    return [
        lambda z, core, x, y: ((z + 2) % nz, core, x, y),
        lambda z, core, x, y: (((z // 2 + nz // 4) * 2 + 1 - z % 2) % nz, core, x, y),
        lambda z, core, x, y: ((z - 2) % nz, core, x, y),
    ]


def to_all(value, axes, peers):
    copies = jnp.broadcast_to(value[None], (peers, *value.shape))
    return lax.all_to_all(copies, axes, 0, 0, tiled=True)


def local(
    cost_tiles, tile_rows, tile_cols, tile_count, source_logmass, target_logmass, target_init
):
    cost = cost_tiles.reshape(cost_tiles.shape[2:])
    rows = tile_rows.reshape(-1)
    cols = tile_cols.reshape(-1)
    count = tile_count.reshape(1, 1)
    srcmass = source_logmass.reshape(-1, LANES)
    tgtmass = target_logmass.reshape(-1, LANES)
    nz = lax.axis_size("z")
    slots = cost.shape[0]

    def f32(*shape):
        return pltpu.VMEM(shape, jnp.float32)

    def keep(x):
        return pltpu.with_memory_space_constraint(x, pltpu.VMEM)

    def far(x):
        return pltpu.with_memory_space_constraint(x, pltpu.HBM)

    full, named, values = f32(LANES, LANES), f32(8, LANES), f32(slots, LANES)
    ids = (pltpu.VMEM((slots, LANES), jnp.int32), values, named)
    anywhere = pl.BlockSpec(memory_space=pl.ANY)
    col_names = None
    for step in range(ITERS):
        sent = f32(slots + 8, LANES) if step == 0 else f32(slots, LANES)
        if step == 0:
            listed, *kept = call(
                first_rows_kernel, "first_rows",
                (far(rows), far(cols), far(cost), far(target_init.reshape(-1, LANES)), count),
                [anywhere] * 4 + [pl.BlockSpec(memory_space=pltpu.SMEM)],
                (sent, f32(*cost.shape), *ids, *ids),
                (
                    f32(*cost.shape),
                    pltpu.SMEM((slots,), jnp.int32),
                    pltpu.SMEM((slots,), jnp.int32),
                    full,
                    pltpu.SemaphoreType.DMA((3,)),
                    pltpu.SemaphoreType.DMA((slots // CHUNK,)),
                    pltpu.VMEM((LANES, LANES), jnp.int32),
                    values,
                    values,
                ),
            )
            tiles_held, row_up, row_same, row_named, col_up, col_same, col_named = (keep(x) for x in kept)
        else:
            listed = call(
                rows_kernel, "rows_half",
                (mine, other, tgtmass, tiles_held, row_up, row_same, row_named, col_up),
                None, (sent,), (values, values),
            )
        parts = exchange(listed, nz, ring_routes(0))
        col_names = parts if step == 0 else col_names
        part = call(ring_kernel, "ring", (*parts, *col_names), None, (full,), ())
        source, listed = call(
            cols_kernel, "cols_half",
            (*exchange(part, nz, ring_routes(1)), srcmass, tiles_held, row_up, col_up, col_same, col_named),
            None, (jax.ShapeDtypeStruct((LANES, LANES), jnp.float32), f32(slots + 8, LANES)),
            (values, values),
        )
        if step < ITERS - 1:
            parts = to_all(listed, "z", nz).reshape(nz, -1, LANES)
            mine = call(spread_kernel, "spread", (parts, parts), None, (full,), (f32(nz, LANES, LANES),))
            other = lax.ppermute(mine, "core", [(0, 1), (1, 0)])
    parts = exchange(listed, nz, pair_routes())
    part = call(ring_kernel, "pair", (*parts, *parts), None, (full,), ())
    target = EPS * tgtmass - BACK * ring_lse2(exchange(part, nz, line_routes(nz)))
    return (source.reshape(-1), target.reshape(-1))


def solution(mesh):
    nrow, ncol = mesh.devices.shape
    cores = 2
    finer = Mesh(mesh.devices.reshape(nrow // cores, cores, ncol), ("z", "core", "col"))
    row = ("z", "core")
    return jax.shard_map(
        local,
        mesh=finer,
        in_specs=(
            P(row, "col", None, None, None),
            P(row, "col", None),
            P(row, "col", None),
            P(row, "col"),
            P(row),
            P("col"),
            P("col"),
        ),
        out_specs=(P(row), P("col")),
        check_vma=False,
    )
```

```python
import jax
import jax.numpy as jnp
import numpy as np
from jax import lax
from jax.experimental import pallas as pl
from jax.experimental.pallas import tpu as pltpu
from jax.sharding import Mesh
from jax.sharding import PartitionSpec as P

ITERS = 2
EPS = 0.1
LN2 = float(np.log(2.0))
UNIT = 1.0 / (EPS * LN2)
BACK = EPS * LN2
NONE = -1.0e30
LANES = 128
SLOTS = 64
RING = 4
CHUNK = 16
AHEAD = 2
LIMIT = 24 << 20


def pieces(x):
    high = x.astype(jnp.bfloat16)
    rest = x - high.astype(jnp.float32)
    middle = rest.astype(jnp.bfloat16)
    low = (rest - middle.astype(jnp.float32)).astype(jnp.bfloat16)
    return high, middle, low


def note_ids(ids, count, upright, same, named, scratch):
    slots = ids.shape[0]
    for s in range(slots):
        one = jnp.full((1, LANES), jnp.where(s < count, ids[s], -1), jnp.int32)
        scratch[pl.ds(s, 1), :] = one
        scratch[pl.ds(slots + s, 1), :] = one
    upright[...] = scratch[:slots, :]
    across = scratch[...].T[:slots, :]
    equal = upright[...] == across
    same[...] = jnp.where(equal, 1.0, 0.0)
    above = lax.broadcasted_iota(jnp.int32, (slots, LANES), 0)
    lane = lax.broadcasted_iota(jnp.int32, (slots, LANES), 1)
    earlier = above < jnp.where(lane < slots, lane, lane - slots)
    again = jnp.max(jnp.where(earlier & equal, 1.0, 0.0), axis=0, keepdims=True)
    once = jnp.where(again > 0.0, -1.0, across[:1, :].astype(jnp.float32))
    named[...] = jnp.broadcast_to(once, named.shape)


def gathered(pot, upright):
    block = lax.broadcasted_iota(jnp.int32, upright.shape, 1)
    pick = jnp.where(block == upright[...], 1.0, 0.0).astype(jnp.bfloat16)
    return jnp.dot(
        jnp.concatenate([pick, pick, pick], axis=1),
        jnp.concatenate(pieces(pot), axis=0),
        preferred_element_type=jnp.float32,
    )


def merged(values, upright, same, out):
    slots = values.shape[0]
    mine = upright[...]
    values[...] = jnp.where(mine >= 0, values[...], 0.0)
    top = jnp.full((slots, LANES), NONE, jnp.float32)
    for s in range(slots):
        hit = mine == upright[pl.ds(s, 1), :]
        top = jnp.maximum(top, jnp.where(hit, values[pl.ds(s, 1), :], NONE))
    high, middle, _ = pieces(jnp.exp2(values[...] - top))
    mass = jnp.dot(
        same[...].astype(jnp.bfloat16),
        jnp.concatenate([high, middle], axis=0),
        preferred_element_type=jnp.float32,
    )
    out[:slots, :] = top + jnp.log2(mass)


def placed(rows, ids):
    block = lax.broadcasted_iota(jnp.int32, (LANES, LANES), 0).astype(jnp.float32)
    ones = jnp.ones((SLOTS, LANES), jnp.bfloat16)
    none = jnp.zeros((SLOTS, LANES), jnp.bfloat16)
    pick = jnp.where(block == ids, 1.0, 0.0).astype(jnp.bfloat16)
    both = jnp.dot(
        jnp.concatenate([pick, pick], axis=1),
        jnp.concatenate(
            [jnp.concatenate([*pieces(rows), none], axis=0), jnp.concatenate([ones, none, none, none], axis=0)],
            axis=1,
        ),
        preferred_element_type=jnp.float32,
    )
    return jnp.where(both[:, LANES:] > 0.5, both[:, :LANES], NONE)


def spread(parts, names, dense):
    top = jnp.full((LANES, LANES), NONE, jnp.float32)
    for d in range(parts.shape[0]):
        value = placed(parts[d, :SLOTS, :], names[d, SLOTS : SLOTS + 1, :])
        dense[d] = value
        top = jnp.maximum(top, value)
    total = jnp.zeros((LANES, LANES), jnp.float32)
    for d in range(parts.shape[0]):
        total = total + jnp.exp2(dense[d] - top)
    return jnp.maximum(top + jnp.log2(total), NONE)


def add_names(named, out):
    if out.shape[0] > SLOTS:
        out[SLOTS:, :] = named[...]


def one_row_tile(part, tile):
    scores = (part - tile).T
    top = jnp.max(scores, axis=0, keepdims=True)
    return top + jnp.log2(jnp.sum(jnp.exp2(scores - top), axis=0, keepdims=True))


def one_col_tile(part, tile):
    upright = jnp.broadcast_to(part, tile.shape).T
    scores = upright - tile
    top = jnp.max(scores, axis=0, keepdims=True)
    return top + jnp.log2(jnp.sum(jnp.exp2(scores - top), axis=0, keepdims=True))


def tiles(tile_lse, cost, picked, values):
    for s in range(cost.shape[0]):
        values[pl.ds(s, 1), :] = tile_lse(picked[pl.ds(s, 1), :], cost[s])


def first_rows_kernel(
    rows_in, cols_in, cost_in, pot_in, count_in,
    out, cost, row_up, row_same, row_named, col_up, col_same, col_named,
    landing, rows, cols, pot, sems, cost_sems, scratch, values, picked,
):
    count = count_in[0, 0]
    small = []
    for k, (src, dst) in enumerate(((cols_in, cols), (rows_in, rows), (pot_in, pot))):
        small.append(pltpu.make_async_copy(src, dst, sems.at[k]))
        small[-1].start()
    chunks = []
    for k in range(cost.shape[0] // CHUNK):
        at = pl.ds(k * CHUNK, CHUNK)
        chunks.append(pltpu.make_async_copy(cost_in.at[at], landing.at[at], cost_sems.at[k]))
        if k < AHEAD:
            pl.when(count > k * CHUNK)(chunks[k].start)
    values[...] = jnp.zeros(values.shape, jnp.float32)
    for copy in small:
        copy.wait()
    note_ids(cols, count, col_up, col_same, col_named, scratch)
    picked[...] = gathered(UNIT * pot[...], col_up)
    note_ids(rows, count, row_up, row_same, row_named, scratch)
    add_names(row_named, out)
    for k, chunk in enumerate(chunks):

        @pl.when(count > k * CHUNK)
        def _():
            chunk.wait()
            if k + AHEAD < len(chunks):
                pl.when(count > (k + AHEAD) * CHUNK)(chunks[k + AHEAD].start)
            for s in range(k * CHUNK, (k + 1) * CHUNK):
                tile = UNIT * landing[s]
                cost[s] = tile
                values[pl.ds(s, 1), :] = one_row_tile(picked[pl.ds(s, 1), :], tile)

    merged(values, row_up, row_same, out)


def rows_kernel(mine, other, logmass, cost, row_up, row_same, row_named, col_up, out, values, picked):
    add_names(row_named, out)
    pot = EPS * logmass[...] - BACK * pair_lse2(mine[...], other[...])
    picked[...] = gathered(UNIT * pot, col_up)
    tiles(one_row_tile, cost, picked, values)
    merged(values, row_up, row_same, out)


def cols_kernel(
    one, two, three, four, logmass, cost, row_up, col_up, col_same, col_named, pot, out, values, picked
):
    add_names(col_named, out)
    pot[...] = EPS * logmass[...] - BACK * ring_lse2([x[...] for x in (one, two, three, four)])
    picked[...] = gathered(UNIT * pot[...], row_up)
    tiles(one_col_tile, cost, picked, values)
    merged(values, col_up, col_same, out)


def ring_lse2(parts):
    top = jnp.maximum(jnp.maximum(parts[0], parts[2]), jnp.maximum(parts[1], parts[3]))
    own, after, across, before = (jnp.exp2(part - top) for part in parts)
    return jnp.maximum(top + jnp.log2((own + across) + (after + before)), NONE)


def ring_kernel(*refs):
    parts, names, out = refs[:4], refs[4:8], refs[8]
    out[...] = ring_lse2([placed(part[:SLOTS, :], name[SLOTS : SLOTS + 1, :]) for part, name in zip(parts, names)])


def spread_kernel(parts, names, out, dense):
    out[...] = spread(parts, names, dense)


def pair_lse2(a, b):
    return jnp.maximum(a, b) + jnp.log2(1.0 + jnp.exp2(-jnp.abs(a - b)))


def call(kernel, name, operands, specs, outs, scratch):
    held = pl.BlockSpec(memory_space=pltpu.VMEM)
    single = len(outs) == 1
    return pl.pallas_call(
        kernel,
        name=name,
        out_shape=outs[0] if single else outs,
        in_specs=[held] * len(operands) if specs is None else specs,
        out_specs=held if single else tuple(held for _ in outs),
        scratch_shapes=scratch,
        compiler_params=pltpu.CompilerParams(vmem_limit_bytes=LIMIT),
    )(*operands)


def exchange(value, nz, routes):
    got = [value]
    for route in routes:
        pairs = []
        for z in range(nz):
            for core in range(2):
                for x in range(RING):
                    for y in range(RING):
                        to = route(z, core, x, y)
                        here = ((z * 2 + core) * RING + x) * RING + y
                        pairs.append((here, ((to[0] * 2 + to[1]) * RING + to[2]) * RING + to[3]))
        got.append(lax.ppermute(value, ("z", "core", "col"), pairs))
    return got


def ring_routes(stage):
    def route(hop):
        def to(z, core, x, y):
            if core == stage:
                return z, core, (x + hop) % RING, y
            return z, core, x, (y + hop) % RING

        return to

    return [route(hop) for hop in (1, 2, 3)]


def pair_routes():
    return [
        lambda z, core, x, y: (z, 1 - core, x, y),
        lambda z, core, x, y: (z ^ 1, core, x, y),
        lambda z, core, x, y: (z ^ 1, 1 - core, x, y),
    ]


def line_routes(nz):
    return [
        lambda z, core, x, y: ((z + 2) % nz, core, x, y),
        lambda z, core, x, y: (((z // 2 + nz // 4) * 2 + 1 - z % 2) % nz, core, x, y),
        lambda z, core, x, y: ((z - 2) % nz, core, x, y),
    ]


def to_all(value, axes, peers):
    copies = jnp.broadcast_to(value[None], (peers, *value.shape))
    return lax.all_to_all(copies, axes, 0, 0, tiled=True)


def local(
    cost_tiles, tile_rows, tile_cols, tile_count, source_logmass, target_logmass, target_init
):
    cost = cost_tiles.reshape(cost_tiles.shape[2:])
    rows = tile_rows.reshape(-1)
    cols = tile_cols.reshape(-1)
    count = tile_count.reshape(1, 1)
    srcmass = source_logmass.reshape(-1, LANES)
    tgtmass = target_logmass.reshape(-1, LANES)
    nz = lax.axis_size("z")
    slots = cost.shape[0]

    def f32(*shape):
        return pltpu.VMEM(shape, jnp.float32)

    def keep(x):
        return pltpu.with_memory_space_constraint(x, pltpu.VMEM)

    def far(x):
        return pltpu.with_memory_space_constraint(x, pltpu.HBM)

    full, named, values = f32(LANES, LANES), f32(8, LANES), f32(slots, LANES)
    ids = (pltpu.VMEM((slots, LANES), jnp.int32), values, named)
    anywhere = pl.BlockSpec(memory_space=pl.ANY)
    col_names = None
    for step in range(ITERS):
        sent = f32(slots + 8, LANES) if step == 0 else f32(slots, LANES)
        if step == 0:
            listed, *kept = call(
                first_rows_kernel, "first_rows",
                (far(rows), far(cols), far(cost), far(target_init.reshape(-1, LANES)), count),
                [anywhere] * 4 + [pl.BlockSpec(memory_space=pltpu.SMEM)],
                (sent, f32(*cost.shape), *ids, *ids),
                (
                    f32(*cost.shape),
                    pltpu.SMEM((slots,), jnp.int32),
                    pltpu.SMEM((slots,), jnp.int32),
                    full,
                    pltpu.SemaphoreType.DMA((3,)),
                    pltpu.SemaphoreType.DMA((slots // CHUNK,)),
                    pltpu.VMEM((LANES, LANES), jnp.int32),
                    values,
                    values,
                ),
            )
            tiles_held, row_up, row_same, row_named, col_up, col_same, col_named = (keep(x) for x in kept)
        else:
            listed = call(
                rows_kernel, "rows_half",
                (mine, other, tgtmass, tiles_held, row_up, row_same, row_named, col_up),
                None, (sent,), (values, values),
            )
        parts = exchange(listed, nz, ring_routes(0))
        col_names = parts if step == 0 else col_names
        part = call(ring_kernel, "ring", (*parts, *col_names), None, (full,), ())
        source, listed = call(
            cols_kernel, "cols_half",
            (*exchange(part, nz, ring_routes(1)), srcmass, tiles_held, row_up, col_up, col_same, col_named),
            None, (jax.ShapeDtypeStruct((LANES, LANES), jnp.float32), f32(slots + 8, LANES)),
            (values, values),
        )
        if step < ITERS - 1:
            parts = to_all(listed, "z", nz).reshape(nz, -1, LANES)
            mine = call(spread_kernel, "spread", (parts, parts), None, (full,), (f32(nz, LANES, LANES),))
            other = lax.ppermute(mine, "core", [(0, 1), (1, 0)])
    parts = exchange(listed, nz, pair_routes())
    part = call(ring_kernel, "pair", (*parts, *parts), None, (full,), ())
    target = EPS * tgtmass - BACK * ring_lse2(exchange(part, nz, line_routes(nz)))
    return (source.reshape(-1), target.reshape(-1))


def solution(mesh):
    nrow, ncol = mesh.devices.shape
    cores = 2
    finer = Mesh(mesh.devices.reshape(nrow // cores, cores, ncol), ("z", "core", "col"))
    row = ("z", "core")
    return jax.shard_map(
        local,
        mesh=finer,
        in_specs=(
            P(row, "col", None, None, None),
            P(row, "col", None),
            P(row, "col", None),
            P(row, "col"),
            P(row),
            P("col"),
            P("col"),
        ),
        out_specs=(P(row), P("col")),
        check_vma=False,
    )
```
